32 devices in a mesh: dp: 4 (over y, x), ctx: 2 (over core), tp: 4 (over z).
Axes of the slice: x: 2, y: 2, z: 4, core: 2. Of those that a mesh axis runs over, the one named last changes fastest.
Arguments:
- tokens: bfloat16 [4096, 1024], P(('dp', 'ctx')), may hold values from -6 to 6
- norm_gain: float32 [1024], replicated, may hold values from 0.5 to 1.5
- gate_weight: bfloat16 [1024, 2048], P(('dp', 'ctx'), 'tp'), may hold values from -0.1875 to 0.1875
- input_weight: bfloat16 [1024, 2048], P(('dp', 'ctx'), 'tp'), may hold values from -0.1875 to 0.1875
- state_weight: bfloat16 [1024, 256], P(('dp', 'ctx'), 'tp'), may hold values from -0.1875 to 0.1875
- step_weight: bfloat16 [1024, 32], P(('dp', 'ctx'), 'tp'), may hold values from -0.1875 to 0.1875
- input_kernel: float32 [4, 2048], P(None, 'tp'), may hold values from -0.5 to 0.5
- input_offset: float32 [2048], P('tp'), may hold values from -0.5 to 0.5
- state_kernel: float32 [4, 256], P(None, 'tp'), may hold values from -0.5 to 0.5
- state_offset: float32 [256], P('tp'), may hold values from -0.5 to 0.5
- step_bias: float32 [32], P('tp'), may hold values from -5.5 to -3.5
- decay_log: float32 [32], P('tp'), may hold values from -4.6 to 1.1
- skip_gain: float32 [32], P('tp'), may hold values from 0.5 to 1.5
- gated_gain: float32 [2048], P('tp'), may hold values from 0.5 to 1.5
- out_weight: bfloat16 [2048, 1024], P('tp', ('dp', 'ctx')), may hold values from -0.125 to 0.125
- cotangent: bfloat16 [4096, 1024], P(('dp', 'ctx')), may hold values from -6 to 6
Outputs:
- block_out: bfloat16 [4096, 1024], P(('dp', 'ctx'))
- grad_tokens: float32 [4096, 1024], P(('dp', 'ctx'))
- grad_norm_gain: float32 [1024], replicated
- grad_gate_weight: float32 [1024, 2048], P(('dp', 'ctx'), 'tp')
- grad_input_weight: float32 [1024, 2048], P(('dp', 'ctx'), 'tp')
- grad_state_weight: float32 [1024, 256], P(('dp', 'ctx'), 'tp')
- grad_step_weight: float32 [1024, 32], P(('dp', 'ctx'), 'tp')
- grad_input_kernel: float32 [4, 2048], P(None, 'tp')
- grad_input_offset: float32 [2048], P('tp')
- grad_state_kernel: float32 [4, 256], P(None, 'tp')
- grad_state_offset: float32 [256], P('tp')
- grad_step_bias: float32 [32], P('tp')
- grad_decay_log: float32 [32], P('tp')
- grad_skip_gain: float32 [32], P('tp')
- grad_gated_gain: float32 [2048], P('tp')
- grad_out_weight: float32 [2048, 1024], P('tp', ('dp', 'ctx'))
The draws below stay inside these ranges and needn't reach their ends.
All inputs are finite; a program needn't handle non-finite values.
Results may differ from the reference program's by a relative error of at most 0.012.
Values may be sent and summed in bfloat16 or wider, within the bound.
A program may use at most 128 MiB of HBM per device.

```python
import jax
import jax.numpy as jnp
from jax import lax

D = 1024
DI = 2048
HEADS = 32
STATE = 128
CONV = 4
STRETCH = 256
SEQ = 1024
TOKENS = 4096


def shard_levels(own_key, dims, split, smallest, top_value):
    gain, own = 1.0, jax.random.fold_in(own_key, 6)
    for position, parts in split:
        draws = jnp.exp(jax.random.uniform(jax.random.fold_in(own, position), (parts,), jnp.float32, smallest / len(split), top_value / len(split)))
        gain = gain * jnp.repeat(draws, dims[position] // parts).reshape([-1 if axis == position else 1 for axis in range(len(dims))])
    return gain


def noise(own_key, dims, width, bound, pieces=(), dtype=jnp.bfloat16):
    drawn = jax.random.normal(own_key, dims, jnp.float32) * width
    if len(pieces) > 0:
        drawn = shard_levels(own_key, dims, pieces, -0.22, 0.18) * drawn
    return jnp.clip(drawn, min=-bound, max=bound).astype(dtype)


def setup_inputs(seed: int = 0) -> dict:
    splits = jax.random.split(jax.random.key(seed), 17)
    return {
        "tokens": noise(splits[0], (TOKENS, D), 1.0, 6.0, ((0, 8),)),
        "norm_gain": jnp.clip(1.0 + 0.1 * jax.random.normal(splits[1], (D,), jnp.float32), 0.5, 1.5),
        "gate_weight": noise(splits[2], (D, DI), D ** -0.5, 0.1875, ((0, 8), (1, 4))),
        "input_weight": noise(splits[3], (D, DI), D ** -0.5, 0.1875, ((0, 8), (1, 4))),
        "state_weight": noise(splits[4], (D, 2 * STATE), D ** -0.5, 0.1875, ((0, 8), (1, 4))),
        "step_weight": noise(splits[5], (D, HEADS), D ** -0.5, 0.1875, ((0, 8), (1, 4))),
        "input_kernel": jnp.clip(jax.random.uniform(splits[6], (CONV, DI), jnp.float32, -0.5, 0.5) * shard_levels(splits[6], (CONV, DI), ((1, 4),), -0.4, 0.0), -0.5, 0.5),
        "input_offset": jnp.clip(jax.random.uniform(splits[7], (DI,), jnp.float32, -0.5, 0.5) * shard_levels(splits[7], (DI,), ((0, 4),), -0.4, 0.0), -0.5, 0.5),
        "state_kernel": jnp.clip(jax.random.uniform(splits[8], (CONV, 2 * STATE), jnp.float32, -0.5, 0.5) * shard_levels(splits[8], (CONV, 2 * STATE), ((1, 4),), -0.4, 0.0), -0.5, 0.5),
        "state_offset": jnp.clip(jax.random.uniform(splits[9], (2 * STATE,), jnp.float32, -0.5, 0.5) * shard_levels(splits[9], (2 * STATE,), ((0, 4),), -0.4, 0.0), -0.5, 0.5),
        "step_bias": jnp.clip(-5.5 + 2.0 * jax.random.uniform(splits[10], (HEADS,), jnp.float32) ** shard_levels(splits[10], (HEADS,), ((0, 4),), -0.2, 0.2), -5.5, -3.5),
        "decay_log": jnp.clip(-4.6 + 5.7 * jax.random.uniform(splits[11], (HEADS,), jnp.float32) ** shard_levels(splits[11], (HEADS,), ((0, 4),), -0.2, 0.2), -4.6, 1.1),
        "skip_gain": jnp.clip(0.5 + 1.0 * jax.random.uniform(splits[12], (HEADS,), jnp.float32) ** shard_levels(splits[12], (HEADS,), ((0, 4),), -0.2, 0.2), 0.5, 1.5),
        "gated_gain": jnp.clip(1.0 + 0.1 * jax.random.normal(splits[13], (DI,), jnp.float32), 0.5, 1.5),
        "out_weight": noise(splits[14], (DI, D), DI ** -0.5, 0.125, ((0, 4), (1, 8))),
        "cotangent": noise(splits[15], (TOKENS, D), 1.0, 6.0, ((0, 8),)),
    }


epsilon = 1e-05
exact_mode = lax.Precision.HIGHEST

@jax.custom_vjp
def low(v):
    return lax.optimization_barrier(v.astype(jnp.bfloat16)).astype(jnp.float32)

@jax.custom_vjp
def low_back(v):
    return v

def low_keep(v):
    return (low(v), None)

def low_pass(kept, grad):
    return (grad,)

def back_keep(v):
    return (v, None)

def back_low(kept, grad):
    return (low(grad),)
low.defvjp(low_keep, low_pass)
low_back.defvjp(back_keep, back_low)

def rms_norm(values, norm_scale):
    meansq = lax.optimization_barrier(jnp.mean(values * values, axis=-1, keepdims=True))
    return values * lax.rsqrt(meansq + epsilon) * norm_scale

def causal_conv(padded, kernel, offset):
    tap_count = kernel.shape[0]
    length = padded.shape[0] - tap_count + 1
    summed = offset[None, :] + kernel[0][None, :] * padded[0:length]
    for tap_index in range(1, tap_count):
        summed = summed + kernel[tap_index][None, :] * padded[tap_index:tap_index + length]
    return jax.nn.silu(summed)

def block_step(carry_state, block_in):
    values, step_sizes, decays, inputs_b, readout_c = block_in
    running = jnp.cumsum(decays, axis=0)
    length = running.shape[0]
    rowpos = lax.broadcasted_iota(jnp.int32, (length, length), 0)
    colpos = lax.broadcasted_iota(jnp.int32, (length, length), 1)
    causal = (rowpos >= colpos)[:, :, None]
    spread = running[:, None, :] - running[None, :, :]
    weights = jnp.exp(jnp.where(causal, spread, -jnp.inf))
    scores = jnp.dot(readout_c, inputs_b.T, precision=exact_mode)
    mixing = weights * scores[:, :, None] * step_sizes[None, :, :]
    within = jnp.einsum('ijh,jhp->ihp', mixing, values, precision=exact_mode)
    carried = jnp.einsum('in,hpn->ihp', readout_c, carry_state, precision=exact_mode) * jnp.exp(running)[:, :, None]
    block_total = running[-1]
    tail_weight = jnp.exp(block_total[None, :] - running) * step_sizes
    fresh_state = jnp.einsum('jh,jn,jhp->hpn', tail_weight, inputs_b, values, precision=exact_mode)
    new_state = jnp.exp(block_total)[:, None, None] * carry_state + fresh_state
    return (new_state, within + carried)

def scan_local(values, step_sizes, decays, inputs_b, readout_c, start):
    length, head_count, headdim = values.shape
    blocks_n = length // STRETCH
    blocks = (values.reshape(blocks_n, STRETCH, head_count, headdim), step_sizes.reshape(blocks_n, STRETCH, head_count), decays.reshape(blocks_n, STRETCH, head_count), inputs_b.reshape(blocks_n, STRETCH, inputs_b.shape[1]), readout_c.reshape(blocks_n, STRETCH, readout_c.shape[1]))
    final_state, outputs = lax.scan(jax.checkpoint(block_step), start, blocks)
    return (outputs.reshape(length, head_count, headdim), final_state)

def forward(tokens, norm_gain, gate_weight, input_weight, state_weight, step_weight, input_kernel, input_offset, state_kernel, state_offset, step_bias, decay_log, skip_gain, gated_gain, out_weight):
    normed = low(rms_norm(tokens, norm_gain))
    gate_val = low_back(jnp.dot(normed, gate_weight, precision=exact_mode))
    input_pre = low_back(jnp.dot(normed, input_weight, precision=exact_mode))
    state_pre = low_back(jnp.dot(normed, state_weight, precision=exact_mode))
    step_pre = low_back(jnp.dot(normed, step_weight, precision=exact_mode))
    row_count = tokens.shape[0]
    seq_count = row_count // SEQ
    rim_rows = input_kernel.shape[0] - 1

    def conv_all(projection, kernel, offset):
        grouped = projection.reshape(seq_count, SEQ, projection.shape[1])
        padded = jnp.pad(grouped, ((0, 0), (rim_rows, 0), (0, 0)))
        convolved = jax.vmap(causal_conv, in_axes=(0, None, None))(padded, kernel, offset)
        return convolved.reshape(row_count, projection.shape[1])
    values = conv_all(input_pre, input_kernel, input_offset)
    states_bc = low(conv_all(state_pre, state_kernel, state_offset))
    head_count = step_weight.shape[1]
    headdim = values.shape[1] // head_count
    nstate = states_bc.shape[1] // 2
    step_sizes = jax.nn.softplus(step_pre + step_bias)
    decays = -step_sizes * jnp.exp(decay_log)
    values_heads = values.reshape(seq_count, SEQ, head_count, headdim)
    zero_state = jnp.zeros((seq_count, head_count, headdim, nstate), jnp.float32)
    scanned, ignored = jax.vmap(scan_local)(values_heads, step_sizes.reshape(seq_count, SEQ, head_count), decays.reshape(seq_count, SEQ, head_count), states_bc[:, :nstate].reshape(seq_count, SEQ, nstate), states_bc[:, nstate:].reshape(seq_count, SEQ, nstate), zero_state)
    scanned = scanned + skip_gain[None, None, :, None] * values_heads
    gated_out = scanned.reshape(row_count, head_count * headdim) * jax.nn.silu(gate_val)
    inv_rms = lax.rsqrt(lax.optimization_barrier(jnp.mean(gated_out * gated_out, axis=1, keepdims=True)) + epsilon)
    scaled = low(gated_out * gated_gain)
    projected = low_back(jnp.dot(scaled, out_weight, precision=exact_mode))
    return tokens + inv_rms * projected

def reference(tokens, norm_gain, gate_weight, input_weight, state_weight, step_weight, input_kernel, input_offset, state_kernel, state_offset, step_bias, decay_log, skip_gain, gated_gain, out_weight, cotangent):
    floats = tuple((argument.astype(jnp.float32) for argument in (tokens, norm_gain, gate_weight, input_weight, state_weight, step_weight, input_kernel, input_offset, state_kernel, state_offset, step_bias, decay_log, skip_gain, gated_gain, out_weight)))
    result, pullback = jax.vjp(forward, *floats)
    gradients = pullback(cotangent.astype(jnp.float32))
    return (result.astype(jnp.bfloat16), gradients[0], gradients[1], gradients[2], gradients[3], gradients[4], gradients[5], gradients[6], gradients[7], gradients[8], gradients[9], gradients[10], gradients[11], gradients[12], gradients[13], gradients[14])
```

```python
import functools

import jax
import jax.numpy as jnp
from jax import lax
from jax.experimental import pallas as pl
from jax.experimental.pallas import tpu as pltpu
from jax.sharding import PartitionSpec as P

DI = 2048
STRETCH = 256


epsilon = 1e-05
exact_mode = lax.Precision.HIGHEST


def shifted(value, axis, steps):
    count = lax.axis_size(axis)
    leading, last = (max(0, -steps), min(count, count - steps))
    return lax.ppermute(value, axis, [(source, source + steps) for source in range(leading, last)])


def prefix(array, axis, combine, identity):
    size, here = (lax.axis_size(axis), lax.axis_index(axis))
    everything = jax.tree.map(lambda part: lax.all_gather(part, axis), array)
    start = jax.tree.map(
        lambda part, zero: jnp.broadcast_to(jnp.asarray(zero, part.dtype), part.shape),
        array,
        identity,
    )

    def lap(k, before):
        reached = k < here
        new = combine(before, jax.tree.map(lambda part: part[k], everything))
        return jax.tree.map(lambda a, b: jnp.where(reached, a, b), new, before)

    return lax.fori_loop(0, size, lap, start)


def prefix_2(array, axis, combine, identity):
    size, here = (lax.axis_size(axis), lax.axis_index(axis))
    everything = jax.tree.map(
        lambda part, kind: lax.all_gather(part.astype(kind), axis),
        array,
        jax.tree.map(lambda a: jnp.bfloat16 if a.dtype == jnp.float32 else a.dtype, array),
    )
    start = jax.tree.map(
        lambda part, zero: jnp.broadcast_to(jnp.asarray(zero, part.dtype), part.shape),
        array,
        identity,
    )

    def lap(k, before):
        at = size - 1 - k
        reached = at > here
        new = combine(
            before, jax.tree.map(lambda part, own: part[at].astype(own.dtype), everything, array)
        )
        return jax.tree.map(lambda a, b: jnp.where(reached, a, b), new, before)

    return lax.fori_loop(0, size, lap, start)


def rms_norm(values, norm_scale):
    meansq = jnp.mean(values * values, axis=-1, keepdims=True)
    return values * lax.rsqrt(meansq + epsilon) * norm_scale


def causal_conv(padded, kernel, offset):
    tap_count = kernel.shape[0]
    length = padded.shape[0] - tap_count + 1
    summed = offset[None, :] + kernel[0][None, :] * padded[0:length]
    for tap_index in range(1, tap_count):
        summed = summed + kernel[tap_index][None, :] * padded[tap_index : tap_index + length]
    return jax.nn.silu(summed)


def block_step(carry_state, block_in):
    values, step_sizes, decays, inputs_b, readout_c = block_in
    running = jnp.cumsum(decays, axis=0)
    length = running.shape[0]
    rowpos = lax.broadcasted_iota(jnp.int32, (length, length), 0)
    colpos = lax.broadcasted_iota(jnp.int32, (length, length), 1)
    causal = (rowpos >= colpos)[:, :, None]
    spread = running[:, None, :] - running[None, :, :]
    weights = jnp.exp(jnp.where(causal, spread, -jnp.inf))
    scores = jnp.dot(readout_c, inputs_b.T, precision=exact_mode)
    mixing = weights * scores[:, :, None] * step_sizes[None, :, :]
    within = jnp.einsum("ijh,jhp->ihp", mixing, values, precision=exact_mode)
    carried = (
        jnp.einsum("in,hpn->ihp", readout_c, carry_state, precision=exact_mode)
        * jnp.exp(running)[:, :, None]
    )
    block_total = running[-1]
    tail_weight = jnp.exp(block_total[None, :] - running) * step_sizes
    fresh_state = jnp.einsum("jh,jn,jhp->hpn", tail_weight, inputs_b, values, precision=exact_mode)
    new_state = jnp.exp(block_total)[:, None, None] * carry_state + fresh_state
    return (new_state, within + carried)


def scan_local(values, step_sizes, decays, inputs_b, readout_c, start):
    length, head_count, headdim = values.shape
    blocks_n = length // STRETCH
    blocks = (
        values.reshape(blocks_n, STRETCH, head_count, headdim),
        step_sizes.reshape(blocks_n, STRETCH, head_count),
        decays.reshape(blocks_n, STRETCH, head_count),
        inputs_b.reshape(blocks_n, STRETCH, inputs_b.shape[1]),
        readout_c.reshape(blocks_n, STRETCH, readout_c.shape[1]),
    )
    final_state, outputs = lax.scan(jax.checkpoint(block_step), start, blocks)
    return (outputs.reshape(length, head_count, headdim), final_state)


def mixer_local(values, step_pre, states_full, gate_val, incoming, step_bias, decay_log, skip_gain):
    length = values.shape[0]
    head_count = step_pre.shape[1]
    headdim = values.shape[1] // head_count
    nstate = states_full.shape[1] // 2
    step_sizes = jax.nn.softplus(step_pre + step_bias)
    decays = -step_sizes * jnp.exp(decay_log)
    values_heads = values.reshape(length, head_count, headdim)
    scanned, final_state = scan_local(
        values_heads, step_sizes, decays, states_full[:, :nstate], states_full[:, nstate:], incoming
    )
    scanned = scanned + skip_gain[None, :, None] * values_heads
    gated_out = scanned.reshape(length, head_count * headdim) * jax.nn.silu(gate_val)
    return (gated_out, final_state)


def forward_chain(earlier, later):
    return (earlier[0] + later[0], jnp.exp(later[0])[:, None, None] * earlier[1] + later[1])


def backward_chain(earlier, later):
    return (earlier[0] + later[0], later[1] + jnp.exp(later[0])[:, None, None] * earlier[1])


def times_transposed(left_side, right_side):
    return lax.dot_general(
        left_side, right_side, (((1,), (1,)), ((), ())), preferred_element_type=jnp.float32
    )


def over_rows(left_side, right_side):
    return lax.dot_general(
        left_side, right_side, (((0,), (0,)), ((), ())), preferred_element_type=jnp.float32
    )


MESH = pl.DeviceIdType.MESH
LANES = 128


def line_up(peers):
    barrier = pltpu.get_barrier_semaphore()
    for peer in peers:
        pl.semaphore_signal(barrier, inc=1, device_id=peer, device_id_type=MESH)
    pl.semaphore_wait(barrier, len(peers))


def send_to(source, target, sends, recvs, peer):
    return pltpu.make_async_remote_copy(
        src_ref=source,
        dst_ref=target,
        send_sem=sends,
        recv_sem=recvs,
        device_id=peer,
        device_id_type=MESH,
    )


def gather_kernel(n, ctxn, x_ref, full_ref, own_sem, send, recv, fsend, frecv):
    here = lax.axis_index("dp") * ctxn + lax.axis_index("ctx")
    half = n // 2
    chip, core = lax.div(here, 2), lax.rem(here, 2)
    rows = x_ref.shape[0]

    def spot(index):
        return {"dp": lax.div(index, ctxn), "ctx": lax.rem(index, ctxn)}

    def at(index):
        return full_ref.at[pl.ds(pl.multiple_of(index * rows, rows), rows)]

    sibling = spot(2 * chip + 1 - core)
    peers = [spot(2 * lax.rem(chip + step, half) + core) for step in range(1, half)]
    line_up([sibling] + peers)
    copies = []
    for step in range(1, half):
        copy = send_to(x_ref, at(here), send.at[step], recv.at[step], peers[step - 1])
        copy.start()
        copies.append(copy)
    beside = send_to(x_ref, at(here), send.at[0], recv.at[0], sibling)
    beside.start()
    own = pltpu.make_async_copy(x_ref, at(here), own_sem)
    own.start()
    passed = []
    for step in range(1, half):
        origin = 2 * lax.rem(chip + half - step, half) + core
        copies[step - 1].wait_recv()
        copy = send_to(at(origin), at(origin), fsend.at[step], frecv.at[step], sibling)
        copy.start()
        passed.append(copy)
    own.wait()
    beside.wait()
    for copy in copies:
        copy.wait_send()
    for copy in passed:
        copy.wait()


def gather_rows(shard, n, ctxn, ident):
    rows, columns = shard.shape
    half = n // 2
    return pl.pallas_call(
        functools.partial(gather_kernel, n, ctxn),
        out_shape=jax.ShapeDtypeStruct((n * rows, columns), shard.dtype),
        in_specs=[pl.BlockSpec(memory_space=pltpu.VMEM)],
        out_specs=pl.BlockSpec(memory_space=pltpu.VMEM),
        scratch_shapes=[pltpu.SemaphoreType.DMA] + [pltpu.SemaphoreType.DMA((half,))] * 4,
        compiler_params=pltpu.CompilerParams(
            collective_id=ident, has_side_effects=True, vmem_limit_bytes=32 * 2**20
        ),
    )(shard)


def spread_kernel(axis, n, x_ref, all_ref, own_sem, send, recv):
    here = lax.axis_index(axis)
    peers = [{axis: lax.rem(here + step, n)} for step in range(1, n)]
    line_up(peers)
    copies = []
    for step in range(1, n):
        copy = send_to(x_ref, all_ref.at[here], send.at[step], recv.at[step], peers[step - 1])
        copy.start()
        copies.append(copy)
    own = pltpu.make_async_copy(x_ref, all_ref.at[here], own_sem)
    own.start()
    own.wait()
    for copy in copies:
        copy.wait()


def spread(array, axis, n, ident):
    return pl.pallas_call(
        functools.partial(spread_kernel, axis, n),
        out_shape=jax.ShapeDtypeStruct((n,) + array.shape, array.dtype),
        in_specs=[pl.BlockSpec(memory_space=pltpu.VMEM)],
        out_specs=pl.BlockSpec(memory_space=pltpu.VMEM),
        scratch_shapes=[pltpu.SemaphoreType.DMA] + [pltpu.SemaphoreType.DMA((n,))] * 2,
        compiler_params=pltpu.CompilerParams(
            collective_id=ident, has_side_effects=True, vmem_limit_bytes=32 * 2**20
        ),
    )(array)


def finish_kernel(
    n,
    ctxn,
    tpn,
    grads_ref,
    part_ref,
    small_ref,
    tokens_ref,
    cot_ref,
    gain_ref,
    dw_ref,
    gt_ref,
    sum_ref,
    total_ref,
    beside_buf,
    out_buf,
    in_buf,
    small_in,
    gain_out,
    gain_in,
    tp_in,
    tp_out,
    tp_all,
    sems,
    small_sems,
    tp_sems,
):
    here = lax.axis_index("dp") * ctxn + lax.axis_index("ctx")
    mine = lax.axis_index("tp")
    half = n // 2
    chip, core = lax.div(here, 2), lax.rem(here, 2)
    rows = dw_ref.shape[0]
    piece = tp_out.shape[0]

    def spot(index):
        return {"dp": lax.div(index, ctxn), "ctx": lax.rem(index, ctxn)}

    def span(index):
        return pl.ds(pl.multiple_of(index * rows, rows), rows)

    def part(index):
        return pl.ds(pl.multiple_of(index * piece, piece), piece)

    sibling = spot(2 * chip + 1 - core)
    group = [spot(lax.rem(here + step, n)) for step in range(1, n)]
    line = [{"tp": lax.rem(mine + step, tpn)} for step in range(1, tpn)]
    line_up(group + line)

    scatter = []
    for step in range(1, tpn):
        copy = send_to(
            part_ref.at[part(lax.rem(mine + step, tpn))],
            tp_in.at[step],
            tp_sems.at[0, step],
            tp_sems.at[1, step],
            line[step - 1],
        )
        copy.start()
        scatter.append(copy)
    beside = []
    for step in list(range(1, half)) + [0]:
        copy = send_to(
            grads_ref.at[span(2 * lax.rem(chip + step, half) + 1 - core)],
            beside_buf.at[step],
            sems.at[0, step],
            sems.at[1, step],
            sibling,
        )
        copy.start()
        beside.append(copy)
    smalls = []
    for step in range(1, n):
        copy = send_to(
            small_ref, small_in.at[here], small_sems.at[0, step], small_sems.at[1, step], group[step - 1]
        )
        copy.start()
        smalls.append(copy)
    small_in[here] = small_ref[...]

    across = []
    for step in range(1, half):
        target = 2 * lax.rem(chip + step, half) + core
        beside[step - 1].wait_recv()
        out_buf[step] = (
            grads_ref[span(target)].astype(jnp.float32) + beside_buf[step].astype(jnp.float32)
        ).astype(jnp.bfloat16)
        copy = send_to(
            out_buf.at[step], in_buf.at[step], sems.at[2, step], sems.at[3, step], spot(target)
        )
        copy.start()
        across.append(copy)
    beside[half - 1].wait_recv()
    dw_ref[...] = grads_ref[span(here)].astype(jnp.float32) + beside_buf[0].astype(jnp.float32)

    for copy in smalls:
        copy.wait_recv()
    total = small_in[0]
    for index in range(1, n):
        total = total + small_in[index]
    sum_ref[...] = total
    gain_out[...] = total[:8]
    gain_in[mine] = total[:8]
    gains = []
    for step in range(1, tpn):
        copy = send_to(
            gain_out, gain_in.at[mine], tp_sems.at[4, step], tp_sems.at[5, step], line[step - 1]
        )
        copy.start()
        gains.append(copy)

    normed_grad = part_ref[part(mine)].astype(jnp.float32)
    for step in range(1, tpn):
        scatter[step - 1].wait_recv()
        normed_grad = normed_grad + tp_in[step].astype(jnp.float32)
    tokens = tokens_ref[part(mine)].astype(jnp.float32)
    inv = lax.rsqrt(jnp.mean(tokens * tokens, axis=-1, keepdims=True) + epsilon)
    scaled = normed_grad * gain_ref[...]
    along = jnp.mean(scaled * tokens, axis=-1, keepdims=True)
    change = (inv * scaled - tokens * (inv * inv * inv * along)).astype(jnp.bfloat16)
    tp_out[...] = change
    collect = []
    for step in range(1, tpn):
        copy = send_to(
            tp_out, tp_all.at[part(mine)], tp_sems.at[2, step], tp_sems.at[3, step], line[step - 1]
        )
        copy.start()
        collect.append(copy)
    gt_ref[part(mine)] = cot_ref[part(mine)].astype(jnp.float32) + change.astype(jnp.float32)

    for step in range(1, half):
        across[step - 1].wait_recv()
        dw_ref[...] += in_buf[step].astype(jnp.float32)
    for copy in gains:
        copy.wait_recv()
    whole = gain_in[0]
    for index in range(1, tpn):
        whole = whole + gain_in[index]
    total_ref[...] = whole
    for step in range(1, tpn):
        collect[step - 1].wait_recv()
        where = part(lax.rem(mine + tpn - step, tpn))
        gt_ref[where] = cot_ref[where].astype(jnp.float32) + tp_all[where].astype(jnp.float32)
    for copy in scatter + beside + smalls + across + gains + collect:
        copy.wait_send()


def finish(grads, part, small, tokens, cotangent, norm_gain, n, ctxn, tpn, ident):
    rows, columns = grads.shape[0] // n, grads.shape[1]
    length, width = tokens.shape
    half = n // 2
    piece = length // tpn
    return pl.pallas_call(
        functools.partial(finish_kernel, n, ctxn, tpn),
        out_shape=(
            jax.ShapeDtypeStruct((rows, columns), jnp.float32),
            jax.ShapeDtypeStruct((length, width), jnp.float32),
            jax.ShapeDtypeStruct(small.shape, jnp.float32),
            jax.ShapeDtypeStruct((8, LANES), jnp.float32),
        ),
        in_specs=[pl.BlockSpec(memory_space=pltpu.VMEM)] * 6,
        out_specs=(pl.BlockSpec(memory_space=pltpu.VMEM),) * 4,
        scratch_shapes=[
            pltpu.VMEM((half, rows, columns), jnp.bfloat16),
            pltpu.VMEM((half, rows, columns), jnp.bfloat16),
            pltpu.VMEM((half, rows, columns), jnp.bfloat16),
            pltpu.VMEM((n,) + small.shape, jnp.float32),
            pltpu.VMEM((8, LANES), jnp.float32),
            pltpu.VMEM((tpn, 8, LANES), jnp.float32),
            pltpu.VMEM((tpn, piece, width), jnp.bfloat16),
            pltpu.VMEM((piece, width), jnp.bfloat16),
            pltpu.VMEM((length, width), jnp.bfloat16),
            pltpu.SemaphoreType.DMA((4, half)),
            pltpu.SemaphoreType.DMA((2, n)),
            pltpu.SemaphoreType.DMA((6, tpn)),
        ],
        compiler_params=pltpu.CompilerParams(
            collective_id=ident, has_side_effects=True, vmem_limit_bytes=48 * 2**20
        ),
    )(grads, part, small, tokens, cotangent, norm_gain.reshape(1, width))


def per_device(
    tokens,
    norm_gain,
    gate_weight,
    input_weight,
    state_weight,
    step_weight,
    input_kernel,
    input_offset,
    state_kernel,
    state_offset,
    step_bias,
    decay_log,
    skip_gain,
    gated_gain,
    out_weight,
    cotangent,
):
    ctxn = lax.axis_size("ctx")
    n, tpn = lax.axis_size("dp") * ctxn, lax.axis_size("tp")
    inner, state_width, heads = input_weight.shape[1], state_weight.shape[1], step_weight.shape[1]
    misc_width = -(-(state_width + heads) // LANES) * LANES
    spare = misc_width - state_width - heads
    shard = jnp.concatenate(
        [
            gate_weight,
            input_weight,
            state_weight,
            step_weight,
            jnp.zeros((gate_weight.shape[0], spare), jnp.bfloat16),
            out_weight.T,
        ],
        axis=1,
    )
    full = gather_rows(shard, n, ctxn, 0)
    edges = (0, inner, 2 * inner, 2 * inner + misc_width, 3 * inner + misc_width)
    full_gate, full_input, full_misc, full_out = (
        full[:, low:high] for low, high in zip(edges[:-1], edges[1:])
    )
    residual_in = tokens.astype(jnp.float32)
    normed_low = rms_norm(residual_in, norm_gain).astype(jnp.bfloat16)
    gate_val = jnp.dot(normed_low, full_gate, preferred_element_type=jnp.float32)
    input_pre = jnp.dot(normed_low, full_input, preferred_element_type=jnp.float32)
    misc_pre = jnp.dot(normed_low, full_misc, preferred_element_type=jnp.float32)
    state_pre = misc_pre[:, :state_width]
    step_pre = misc_pre[:, state_width : state_width + heads]
    length = residual_in.shape[0]
    rim_rows = input_kernel.shape[0] - 1
    rim_input, rim_state = shifted(
        (input_pre[length - rim_rows :], state_pre[length - rim_rows :]), "ctx", 1
    )
    values, input_pull = jax.vjp(
        causal_conv, jnp.concatenate([rim_input, input_pre], axis=0), input_kernel, input_offset
    )
    state_act, state_pull = jax.vjp(
        causal_conv, jnp.concatenate([rim_state, state_pre], axis=0), state_kernel, state_offset
    )
    states_full = lax.all_gather(state_act.astype(jnp.bfloat16), "tp", axis=1, tiled=True).astype(
        jnp.float32
    )
    head_count = step_pre.shape[1]
    headdim = values.shape[1] // head_count
    nstate = states_full.shape[1] // 2
    readout_c = states_full[:, nstate:]
    step_sizes = jax.nn.softplus(step_pre + step_bias)
    decays = -step_sizes * jnp.exp(decay_log)
    values_heads = values.reshape(length, head_count, headdim)
    zero_state = jnp.zeros((head_count, headdim, nstate), jnp.float32)
    local_out, local_end = scan_local(
        values_heads, step_sizes, decays, states_full[:, :nstate], readout_c, zero_state
    )
    log_decay = jnp.sum(decays, axis=0)
    ignored_log, incoming = prefix(
        (log_decay, local_end),
        "ctx",
        forward_chain,
        (jnp.zeros_like(log_decay), jnp.zeros_like(local_end)),
    )
    running = jnp.cumsum(decays, axis=0)
    carried = (
        jnp.einsum("tn,hpn->thp", readout_c, incoming, precision=exact_mode)
        * jnp.exp(running)[:, :, None]
    )
    scanned = local_out + carried + skip_gain[None, :, None] * values_heads
    gate_silu = jax.nn.silu(gate_val)
    gated_out = scanned.reshape(length, head_count * headdim) * gate_silu
    scaled_low = (gated_out * gated_gain).astype(jnp.bfloat16)
    partial_out = times_transposed(scaled_low, full_out)
    upstream = cotangent.astype(jnp.float32)
    stats = jnp.stack(
        [jnp.sum(gated_out * gated_out, axis=1), jnp.sum(upstream * partial_out, axis=1)]
    )
    stats = jnp.sum(spread(stats, "tp", tpn, 1), axis=0)
    projected = lax.psum(partial_out.astype(jnp.bfloat16), "tp").astype(jnp.float32)
    inv_rms = lax.rsqrt(stats[0] / DI + epsilon)
    block_out = (residual_in + inv_rms[:, None] * projected).astype(jnp.bfloat16)
    proj_grad = (inv_rms[:, None] * upstream).astype(jnp.bfloat16)
    rms_grad = -0.5 * inv_rms * inv_rms * inv_rms * stats[1] / DI
    scaled_grad = jnp.dot(proj_grad, full_out, preferred_element_type=jnp.float32)
    grad_gated_gain = jnp.sum(scaled_grad * gated_out, axis=0)
    gated_grad = scaled_grad * gated_gain + 2.0 * rms_grad[:, None] * gated_out
    heads_grad = (gated_grad * gate_silu).reshape(length, head_count, headdim)
    direct = jnp.einsum(
        "th,tn,thp->hpn", jnp.exp(running), readout_c, heads_grad, precision=exact_mode
    )
    ignored_back, chain_grad = prefix_2(
        (log_decay, direct),
        "ctx",
        backward_chain,
        (jnp.zeros_like(log_decay), jnp.zeros_like(direct)),
    )
    ignored_out, mixer_pull = jax.vjp(
        mixer_local,
        values,
        step_pre,
        states_full,
        gate_val,
        incoming,
        step_bias,
        decay_log,
        skip_gain,
    )
    (
        values_grad,
        step_grad,
        states_grad,
        gate_grad,
        start_grad,
        step_bias_grad,
        decay_grad,
        skip_grad,
    ) = mixer_pull((gated_grad, chain_grad))
    state_mine = lax.psum_scatter(states_grad, "tp", scatter_dimension=1, tiled=True)
    input_ext_grad, input_kernel_grad, input_offset_grad = input_pull(values_grad)
    state_ext_grad, state_kernel_grad, state_offset_grad = state_pull(state_mine)
    back_input, back_state = shifted(
        (input_ext_grad[:rim_rows], state_ext_grad[:rim_rows]), "ctx", -1
    )
    input_low = (
        input_ext_grad[rim_rows:] + jnp.pad(back_input, ((length - rim_rows, 0), (0, 0)))
    ).astype(jnp.bfloat16)
    state_low = (
        state_ext_grad[rim_rows:] + jnp.pad(back_state, ((length - rim_rows, 0), (0, 0)))
    ).astype(jnp.bfloat16)
    gate_low = gate_grad.astype(jnp.bfloat16)
    step_low = step_grad.astype(jnp.bfloat16)
    misc_low = jnp.concatenate(
        [state_low, step_low, jnp.zeros((length, spare), jnp.bfloat16)], axis=1
    )
    normed_part = (
        times_transposed(gate_low, full_gate)
        + times_transposed(input_low, full_input)
        + times_transposed(misc_low, full_misc)
    )
    grads = jnp.concatenate(
        [
            over_rows(normed_low, gate_low).astype(jnp.bfloat16),
            over_rows(normed_low, input_low).astype(jnp.bfloat16),
            over_rows(normed_low, misc_low).astype(jnp.bfloat16),
            over_rows(proj_grad, scaled_low).astype(jnp.bfloat16),
        ],
        axis=1,
    )
    inv_in = lax.rsqrt(jnp.mean(residual_in * residual_in, axis=-1, keepdims=True) + epsilon)
    gain_part = jnp.sum(normed_part * (residual_in * inv_in), axis=0)
    pieces = (
        gain_part,
        input_kernel_grad,
        input_offset_grad,
        state_kernel_grad,
        state_offset_grad,
        step_bias_grad,
        decay_grad,
        skip_grad,
        grad_gated_gain,
    )
    count = sum(array.size for array in pieces)
    padded = -(-count // (8 * LANES)) * 8 * LANES
    small = jnp.concatenate(
        [array.reshape(-1) for array in pieces] + [jnp.zeros((padded - count,), jnp.float32)]
    ).reshape(padded // LANES, LANES)
    weight_sums, grad_tokens, small_sum, gain_sum = finish(
        grads,
        normed_part.astype(jnp.bfloat16),
        small,
        tokens,
        cotangent,
        norm_gain,
        n,
        ctxn,
        tpn,
        2,
    )
    small_sum = small_sum.reshape(-1)
    sums, start = [], 0
    for array in pieces:
        sums.append(small_sum[start : start + array.size].reshape(array.shape))
        start += array.size
    misc_start = 2 * inner
    return (
        block_out,
        grad_tokens,
        gain_sum.reshape(-1),
        weight_sums[:, :inner],
        weight_sums[:, inner : 2 * inner],
        weight_sums[:, misc_start : misc_start + state_width],
        weight_sums[:, misc_start + state_width : misc_start + state_width + heads],
        *sums[1:],
        weight_sums[:, edges[3] :].T,
    )


def solution(mesh):
    placed = (
        P(("dp", "ctx"), None),
        P(),
        P(("dp", "ctx"), "tp"),
        P(("dp", "ctx"), "tp"),
        P(("dp", "ctx"), "tp"),
        P(("dp", "ctx"), "tp"),
        P(None, "tp"),
        P("tp"),
        P(None, "tp"),
        P("tp"),
        P("tp"),
        P("tp"),
        P("tp"),
        P("tp"),
        P("tp", ("dp", "ctx")),
        P(("dp", "ctx"), None),
    )
    return jax.shard_map(
        per_device,
        mesh=mesh,
        in_specs=placed,
        out_specs=(
            P(("dp", "ctx"), None),
            P(("dp", "ctx"), None),
            P(),
            P(("dp", "ctx"), "tp"),
            P(("dp", "ctx"), "tp"),
            P(("dp", "ctx"), "tp"),
            P(("dp", "ctx"), "tp"),
            P(None, "tp"),
            P("tp"),
            P(None, "tp"),
            P("tp"),
            P("tp"),
            P("tp"),
            P("tp"),
            P("tp"),
            P("tp", ("dp", "ctx")),
        ),
        check_vma=False,
    )
```

```python
import functools

import jax
import jax.numpy as jnp
from jax import lax
from jax.experimental import pallas as pl
from jax.experimental.pallas import tpu as pltpu
from jax.sharding import PartitionSpec as P

DI = 2048
STRETCH = 256


epsilon = 1e-05
exact_mode = lax.Precision.HIGHEST


def shifted(value, axis, steps):
    count = lax.axis_size(axis)
    leading, last = (max(0, -steps), min(count, count - steps))
    return lax.ppermute(value, axis, [(source, source + steps) for source in range(leading, last)])


def chained(log_decay, state, axis, combine, backward, ident):
    size, here = (lax.axis_size(axis), lax.axis_index(axis))
    rows, nstate = state.shape
    heads = log_decay.shape[0]
    packed = jnp.concatenate(
        [state, jnp.broadcast_to(log_decay[:, None], (heads, nstate)).astype(state.dtype)]
    )
    everything = spread(packed, axis, size, ident).astype(jnp.float32)
    logs = everything[:, rows:, 0]
    states = everything[:, :rows].reshape(size, heads, rows // heads, nstate)
    before = (jnp.zeros((heads,), jnp.float32), jnp.zeros(states.shape[1:], jnp.float32))
    for k in range(size):
        at = size - 1 - k if backward else k
        reached = at > here if backward else at < here
        new = combine(before, (logs[at], states[at]))
        before = jax.tree.map(lambda a, b: jnp.where(reached, a, b), new, before)
    return before[1].reshape(rows, nstate)


def rms_norm(values, norm_scale):
    meansq = jnp.mean(values * values, axis=-1, keepdims=True)
    return values * lax.rsqrt(meansq + epsilon) * norm_scale


def causal_conv(padded, kernel, offset):
    tap_count = kernel.shape[0]
    length = padded.shape[0] - tap_count + 1
    summed = offset[None, :] + kernel[0][None, :] * padded[0:length]
    for tap_index in range(1, tap_count):
        summed = summed + kernel[tap_index][None, :] * padded[tap_index : tap_index + length]
    return jax.nn.silu(summed)


def forward_chain(earlier, later):
    return (earlier[0] + later[0], jnp.exp(later[0])[:, None, None] * earlier[1] + later[1])


def backward_chain(earlier, later):
    return (earlier[0] + later[0], later[1] + jnp.exp(later[0])[:, None, None] * earlier[1])


def times_transposed(left_side, right_side):
    return lax.dot_general(
        left_side, right_side, (((1,), (1,)), ((), ())), preferred_element_type=jnp.float32
    )


def over_rows(left_side, right_side):
    return lax.dot_general(
        left_side, right_side, (((0,), (0,)), ((), ())), preferred_element_type=jnp.float32
    )


MESH = pl.DeviceIdType.MESH
LANES = 128


def line_up(peers):
    barrier = pltpu.get_barrier_semaphore()
    for peer in peers:
        pl.semaphore_signal(barrier, inc=1, device_id=peer, device_id_type=MESH)
    pl.semaphore_wait(barrier, len(peers))


def send_to(source, target, sends, recvs, peer):
    return pltpu.make_async_remote_copy(
        src_ref=source,
        dst_ref=target,
        send_sem=sends,
        recv_sem=recvs,
        device_id=peer,
        device_id_type=MESH,
    )


def gather_kernel(n, ctxn, x_ref, full_ref, own_sem, send, recv, fsend, frecv):
    here = lax.axis_index("dp") * ctxn + lax.axis_index("ctx")
    half = n // 2
    chip, core = lax.div(here, 2), lax.rem(here, 2)
    rows = x_ref.shape[0]

    def spot(index):
        return {"dp": lax.div(index, ctxn), "ctx": lax.rem(index, ctxn)}

    def at(index):
        return full_ref.at[pl.ds(pl.multiple_of(index * rows, rows), rows)]

    sibling = spot(2 * chip + 1 - core)
    peers = [spot(2 * lax.rem(chip + step, half) + core) for step in range(1, half)]
    line_up([sibling] + peers)
    copies = []
    for step in range(1, half):
        copy = send_to(x_ref, at(here), send.at[step], recv.at[step], peers[step - 1])
        copy.start()
        copies.append(copy)
    beside = send_to(x_ref, at(here), send.at[0], recv.at[0], sibling)
    beside.start()
    own = pltpu.make_async_copy(x_ref, at(here), own_sem)
    own.start()
    passed = []
    for step in range(1, half):
        origin = 2 * lax.rem(chip + half - step, half) + core
        copies[step - 1].wait_recv()
        copy = send_to(at(origin), at(origin), fsend.at[step], frecv.at[step], sibling)
        copy.start()
        passed.append(copy)
    own.wait()
    beside.wait()
    for copy in copies:
        copy.wait_send()
    for copy in passed:
        copy.wait()


def gather_rows(shard, n, ctxn, ident):
    rows, columns = shard.shape
    half = n // 2
    return pl.pallas_call(
        functools.partial(gather_kernel, n, ctxn),
        out_shape=jax.ShapeDtypeStruct((n * rows, columns), shard.dtype),
        in_specs=[pl.BlockSpec(memory_space=pltpu.VMEM)],
        out_specs=pl.BlockSpec(memory_space=pltpu.VMEM),
        scratch_shapes=[pltpu.SemaphoreType.DMA] + [pltpu.SemaphoreType.DMA((half,))] * 4,
        compiler_params=pltpu.CompilerParams(
            collective_id=ident, has_side_effects=True, vmem_limit_bytes=10 * 2**20
        ),
    )(shard)


def spread_kernel(axis, n, x_ref, all_ref, own_sem, send, recv):
    here = lax.axis_index(axis)
    peers = [{axis: lax.rem(here + step, n)} for step in range(1, n)]
    line_up(peers)
    copies = []
    for step in range(1, n):
        copy = send_to(x_ref, all_ref.at[here], send.at[step], recv.at[step], peers[step - 1])
        copy.start()
        copies.append(copy)
    own = pltpu.make_async_copy(x_ref, all_ref.at[here], own_sem)
    own.start()
    own.wait()
    for copy in copies:
        copy.wait()


def spread(array, axis, n, ident):
    return pl.pallas_call(
        functools.partial(spread_kernel, axis, n),
        out_shape=jax.ShapeDtypeStruct((n,) + array.shape, array.dtype),
        in_specs=[pl.BlockSpec(memory_space=pltpu.VMEM)],
        out_specs=pl.BlockSpec(memory_space=pltpu.VMEM),
        scratch_shapes=[pltpu.SemaphoreType.DMA] + [pltpu.SemaphoreType.DMA((n,))] * 2,
        compiler_params=pltpu.CompilerParams(
            collective_id=ident, has_side_effects=True, vmem_limit_bytes=10 * 2**20
        ),
    )(array)


def finish_kernel(
    n,
    ctxn,
    tpn,
    grads_ref,
    part_ref,
    small_ref,
    tokens_ref,
    cot_ref,
    gain_ref,
    dw_ref,
    gt_ref,
    sum_ref,
    total_ref,
    beside_buf,
    out_buf,
    in_buf,
    small_in,
    gain_out,
    gain_in,
    tp_in,
    tp_out,
    tp_all,
    sems,
    small_sems,
    tp_sems,
):
    here = lax.axis_index("dp") * ctxn + lax.axis_index("ctx")
    mine = lax.axis_index("tp")
    half = n // 2
    chip, core = lax.div(here, 2), lax.rem(here, 2)
    rows = dw_ref.shape[0]
    piece = tp_out.shape[0]

    def spot(index):
        return {"dp": lax.div(index, ctxn), "ctx": lax.rem(index, ctxn)}

    def span(index):
        return pl.ds(pl.multiple_of(index * rows, rows), rows)

    def part(index):
        return pl.ds(pl.multiple_of(index * piece, piece), piece)

    sibling = spot(2 * chip + 1 - core)
    group = [spot(lax.rem(here + step, n)) for step in range(1, n)]
    line = [{"tp": lax.rem(mine + step, tpn)} for step in range(1, tpn)]
    line_up(group + line)

    scatter = []
    for step in range(1, tpn):
        copy = send_to(
            part_ref.at[part(lax.rem(mine + step, tpn))],
            tp_in.at[step],
            tp_sems.at[0, step],
            tp_sems.at[1, step],
            line[step - 1],
        )
        copy.start()
        scatter.append(copy)
    beside = []
    for step in list(range(1, half)) + [0]:
        copy = send_to(
            grads_ref.at[span(2 * lax.rem(chip + step, half) + 1 - core)],
            beside_buf.at[step],
            sems.at[0, step],
            sems.at[1, step],
            sibling,
        )
        copy.start()
        beside.append(copy)
    smalls = []
    for step in range(1, n):
        copy = send_to(
            small_ref, small_in.at[here], small_sems.at[0, step], small_sems.at[1, step], group[step - 1]
        )
        copy.start()
        smalls.append(copy)
    small_in[here] = small_ref[...]

    across = []
    for step in range(1, half):
        target = 2 * lax.rem(chip + step, half) + core
        beside[step - 1].wait_recv()
        out_buf[step] = (
            grads_ref[span(target)].astype(jnp.float32) + beside_buf[step].astype(jnp.float32)
        ).astype(jnp.bfloat16)
        copy = send_to(
            out_buf.at[step], in_buf.at[step], sems.at[2, step], sems.at[3, step], spot(target)
        )
        copy.start()
        across.append(copy)
    beside[half - 1].wait_recv()
    dw_ref[...] = grads_ref[span(here)].astype(jnp.float32) + beside_buf[0].astype(jnp.float32)

    for copy in smalls:
        copy.wait_recv()
    total = small_in[0]
    for index in range(1, n):
        total = total + small_in[index]
    sum_ref[...] = total
    gain_out[...] = total[:8]
    gain_in[mine] = total[:8]
    gains = []
    for step in range(1, tpn):
        copy = send_to(
            gain_out, gain_in.at[mine], tp_sems.at[4, step], tp_sems.at[5, step], line[step - 1]
        )
        copy.start()
        gains.append(copy)

    normed_grad = part_ref[part(mine)].astype(jnp.float32)
    for step in range(1, tpn):
        scatter[step - 1].wait_recv()
        normed_grad = normed_grad + tp_in[step].astype(jnp.float32)
    tokens = tokens_ref[part(mine)].astype(jnp.float32)
    inv = lax.rsqrt(jnp.mean(tokens * tokens, axis=-1, keepdims=True) + epsilon)
    scaled = normed_grad * gain_ref[...]
    along = jnp.mean(scaled * tokens, axis=-1, keepdims=True)
    change = (inv * scaled - tokens * (inv * inv * inv * along)).astype(jnp.bfloat16)
    tp_out[...] = change
    collect = []
    for step in range(1, tpn):
        copy = send_to(
            tp_out, tp_all.at[part(mine)], tp_sems.at[2, step], tp_sems.at[3, step], line[step - 1]
        )
        copy.start()
        collect.append(copy)
    gt_ref[part(mine)] = cot_ref[part(mine)].astype(jnp.float32) + change.astype(jnp.float32)

    for step in range(1, half):
        across[step - 1].wait_recv()
        dw_ref[...] += in_buf[step].astype(jnp.float32)
    for copy in gains:
        copy.wait_recv()
    whole = gain_in[0]
    for index in range(1, tpn):
        whole = whole + gain_in[index]
    total_ref[...] = whole
    for step in range(1, tpn):
        collect[step - 1].wait_recv()
        where = part(lax.rem(mine + tpn - step, tpn))
        gt_ref[where] = cot_ref[where].astype(jnp.float32) + tp_all[where].astype(jnp.float32)
    for copy in scatter + beside + smalls + across + gains + collect:
        copy.wait_send()


def finish(grads, part, small, tokens, cotangent, norm_gain, n, ctxn, tpn, ident):
    rows, columns = grads.shape[0] // n, grads.shape[1]
    length, width = tokens.shape
    half = n // 2
    piece = length // tpn
    return pl.pallas_call(
        functools.partial(finish_kernel, n, ctxn, tpn),
        out_shape=(
            jax.ShapeDtypeStruct((rows, columns), jnp.float32),
            jax.ShapeDtypeStruct((length, width), jnp.float32),
            jax.ShapeDtypeStruct(small.shape, jnp.float32),
            jax.ShapeDtypeStruct((8, LANES), jnp.float32),
        ),
        in_specs=[pl.BlockSpec(memory_space=pltpu.VMEM)] * 6,
        out_specs=(pl.BlockSpec(memory_space=pltpu.VMEM),) * 4,
        scratch_shapes=[
            pltpu.VMEM((half, rows, columns), jnp.bfloat16),
            pltpu.VMEM((half, rows, columns), jnp.bfloat16),
            pltpu.VMEM((half, rows, columns), jnp.bfloat16),
            pltpu.VMEM((n,) + small.shape, jnp.float32),
            pltpu.VMEM((8, LANES), jnp.float32),
            pltpu.VMEM((tpn, 8, LANES), jnp.float32),
            pltpu.VMEM((tpn, piece, width), jnp.bfloat16),
            pltpu.VMEM((piece, width), jnp.bfloat16),
            pltpu.VMEM((length, width), jnp.bfloat16),
            pltpu.SemaphoreType.DMA((4, half)),
            pltpu.SemaphoreType.DMA((2, n)),
            pltpu.SemaphoreType.DMA((6, tpn)),
        ],
        compiler_params=pltpu.CompilerParams(
            collective_id=ident, has_side_effects=True, vmem_limit_bytes=28 * 2**20
        ),
    )(grads, part, small, tokens, cotangent, norm_gain.reshape(1, width))


def swap_kernel(axis, n, x_ref, all_ref, own_sem, send, recv):
    here = lax.axis_index(axis)
    peers = [{axis: lax.rem(here + step, n)} for step in range(1, n)]
    line_up(peers)
    copies = []
    for step in range(1, n):
        copy = send_to(
            x_ref.at[lax.rem(here + step, n)],
            all_ref.at[here],
            send.at[step],
            recv.at[step],
            peers[step - 1],
        )
        copy.start()
        copies.append(copy)
    own = pltpu.make_async_copy(x_ref.at[here], all_ref.at[here], own_sem)
    own.start()
    own.wait()
    for copy in copies:
        copy.wait()


def swap(array, axis, n, ident):
    return pl.pallas_call(
        functools.partial(swap_kernel, axis, n),
        out_shape=jax.ShapeDtypeStruct(array.shape, array.dtype),
        in_specs=[pl.BlockSpec(memory_space=pltpu.VMEM)],
        out_specs=pl.BlockSpec(memory_space=pltpu.VMEM),
        scratch_shapes=[pltpu.SemaphoreType.DMA] + [pltpu.SemaphoreType.DMA((n,))] * 2,
        compiler_params=pltpu.CompilerParams(
            collective_id=ident, has_side_effects=True, vmem_limit_bytes=10 * 2**20
        ),
    )(array)


def mm(left, right, dims):
    return lax.dot_general(left, right, (dims, ((), ())), preferred_element_type=jnp.float32)


def widen(columns, width):
    rows, heads = columns.shape
    return jnp.concatenate(
        [jnp.broadcast_to(columns[:, h : h + 1], (rows, width)) for h in range(heads)], axis=1
    )


def tallen(row, width, lanes):
    return jnp.concatenate(
        [jnp.broadcast_to(row[:, h : h + 1], (width, lanes)) for h in range(row.shape[1])], axis=0
    )


def per_head(wide, heads):
    width = wide.shape[1] // heads
    return jnp.concatenate(
        [
            jnp.sum(wide[:, h * width : (h + 1) * width], axis=1, keepdims=True)
            for h in range(heads)
        ],
        axis=1,
    )


def decay_matrix(run, run_row, h, causal):
    return jnp.exp(jnp.where(causal, run[:, h : h + 1] - run_row[h : h + 1, :], -1e30))


def causal_mask(size):
    down = lax.broadcasted_iota(jnp.int32, (size, size), 0)
    right = lax.broadcasted_iota(jnp.int32, (size, size), 1)
    return down >= right


def scan_kernel(
    heads,
    x_ref,
    gate_ref,
    bc_ref,
    run_ref,
    run_row_ref,
    dt_ref,
    dt_row_ref,
    start_ref,
    skip_ref,
    gain_ref,
    scanned_ref,
    scaled_ref,
    square_ref,
    kept_ref,
    state,
):
    low = jnp.bfloat16

    @pl.when(pl.program_id(0) == 0)
    def _():
        state[...] = start_ref[...]

    size, inner = x_ref.shape
    width = inner // heads
    nstate = bc_ref.shape[1] // 2
    b, c = bc_ref[:, :nstate], bc_ref[:, nstate:]
    run, run_row = run_ref[...], run_row_ref[...]
    x = x_ref[...]
    x_low = x.astype(low)
    causal = causal_mask(size)
    scores = mm(c, b, ((1,), (1,)))
    held = state[...].astype(low)
    kept_ref[0] = held
    carried = mm(c, held, ((1,), (1,))) * widen(jnp.exp(run), width)
    within = []
    for h in range(heads):
        mixing = decay_matrix(run, run_row, h, causal) * scores * dt_row_ref[h : h + 1, :]
        within.append(mm(mixing.astype(low), x_low[:, h * width : (h + 1) * width], ((1,), (0,))))
    scanned = carried + jnp.concatenate(within, axis=1) + skip_ref[...] * x
    scanned_ref[...] = scanned
    total = run[size - 1 :, :]
    tail = jnp.exp(total - run) * dt_ref[...]
    fresh = mm((x * widen(tail, width)).astype(low), b, ((0,), (0,)))
    state[...] = tallen(jnp.exp(total), width, nstate) * state[...] + fresh
    gate = gate_ref[...]
    gated = scanned * (gate * jax.nn.sigmoid(gate))
    scaled_ref[...] = (gated * gain_ref[...]).astype(low)
    square_ref[...] = jnp.sum(gated * gated, axis=1, keepdims=True)


def scan_forward(x, gate, bc, run, run_row, dt, dt_row, start, skip, gain, heads):
    length, inner = x.shape
    nstate = bc.shape[1] // 2
    size = STRETCH
    wide = pl.BlockSpec((size, inner), lambda i: (i, 0))
    thin = pl.BlockSpec((size, heads), lambda i: (i, 0))
    flat = pl.BlockSpec((heads, size), lambda i: (0, i))
    row = pl.BlockSpec((1, inner), lambda i: (0, 0))
    return pl.pallas_call(
        functools.partial(scan_kernel, heads),
        grid=(length // size,),
        out_shape=(
            jax.ShapeDtypeStruct((length, inner), jnp.float32),
            jax.ShapeDtypeStruct((length, inner), jnp.bfloat16),
            jax.ShapeDtypeStruct((length, 1), jnp.float32),
            jax.ShapeDtypeStruct((length // size, inner, nstate), jnp.bfloat16),
        ),
        in_specs=[
            wide,
            wide,
            pl.BlockSpec((size, 2 * nstate), lambda i: (i, 0)),
            thin,
            flat,
            thin,
            flat,
            pl.BlockSpec((inner, nstate), lambda i: (0, 0)),
            row,
            row,
        ],
        out_specs=(
            wide,
            wide,
            pl.BlockSpec((size, 1), lambda i: (i, 0)),
            pl.BlockSpec((1, inner, nstate), lambda i: (i, 0, 0)),
        ),
        scratch_shapes=[pltpu.VMEM((inner, nstate), jnp.float32)],
        compiler_params=pltpu.CompilerParams(
            dimension_semantics=("arbitrary",), vmem_limit_bytes=28 * 2**20
        ),
    )(x, gate, bc, run, run_row, dt, dt_row, start, skip, gain)


def back_kernel(
    heads,
    x_ref,
    dy_ref,
    bc_ref,
    run_ref,
    run_row_ref,
    dt_ref,
    dt_row_ref,
    end_ref,
    kept_ref,
    skip_ref,
    dx_ref,
    dbc_ref,
    ddt_ref,
    ddecay_ref,
    state,
):
    low = jnp.bfloat16

    @pl.when(pl.program_id(0) == 0)
    def _():
        state[...] = end_ref[...]

    size, inner = x_ref.shape
    width = inner // heads
    nstate = bc_ref.shape[1] // 2
    b, c = bc_ref[:, :nstate], bc_ref[:, nstate:]
    run, run_row, dt = run_ref[...], run_row_ref[...], dt_ref[...]
    x, dy = x_ref[...], dy_ref[...]
    x_low, dy_low = x.astype(low), dy.astype(low)
    causal = causal_mask(size)
    scores = mm(c, b, ((1,), (1,)))
    held = kept_ref[0]
    ds = state[...]
    ds_low = ds.astype(low)

    grown = widen(jnp.exp(run), width)
    dy_grown = dy * grown
    dy_grown_low = dy_grown.astype(low)
    drun = per_head(dy_grown * mm(c, held, ((1,), (1,))), heads)
    dc = mm(dy_grown_low, held, ((1,), (0,)))
    total = run[size - 1 :, :]
    left = jnp.exp(total - run)
    fade = widen(left, width)
    spare = widen(left * dt, width)
    pulled = mm(b, ds_low, ((1,), (1,)))
    db = mm((x * spare).astype(low), ds_low, ((1,), (0,)))
    tail_grad = per_head(x * fade * pulled, heads)
    out_tail = tail_grad * dt
    drun = drun - out_tail
    shrink = tallen(jnp.exp(total), width, nstate)
    lost = jnp.sum(shrink * ds * held.astype(jnp.float32), axis=1, keepdims=True)
    dtotal = jnp.concatenate(
        [
            jnp.sum(lost[h * width : (h + 1) * width], axis=0, keepdims=True)
            for h in range(heads)
        ],
        axis=1,
    ) + jnp.sum(out_tail, axis=0, keepdims=True)
    state[...] = shrink * ds + mm(dy_grown_low, c, ((0,), (0,)))

    dscores = jnp.zeros((size, size), jnp.float32)
    rows, columns, dx = [], [], []
    for h in range(heads):
        lanes = slice(h * width, (h + 1) * width)
        fall = decay_matrix(run, run_row, h, causal)
        dt_row = dt_row_ref[h : h + 1, :]
        products = mm(dy_low[:, lanes], x_low[:, lanes], ((1,), (1,))) * fall
        dscores = dscores + products * dt_row
        terms = products * scores
        columns.append(jnp.sum(terms, axis=0, keepdims=True))
        rows.append(jnp.sum(terms * dt_row, axis=1, keepdims=True))
        mixing = (fall * scores * dt_row).astype(low)
        dx.append(mm(mixing, dy_low[:, lanes], ((0,), (0,))))
    dx_ref[...] = jnp.concatenate(dx, axis=1) + spare * pulled + skip_ref[...] * dy
    dscores = dscores.astype(low)
    dbc_ref[:, :nstate] = db + mm(dscores, c, ((0,), (0,)))
    dbc_ref[:, nstate:] = dc + mm(dscores, b, ((1,), (0,)))
    column = jnp.concatenate(columns, axis=0).T
    ddt_ref[...] = column + tail_grad
    drun = drun + jnp.concatenate(rows, axis=1) - column * dt
    later = jnp.where(causal, 1.0, 0.0)
    ddecay_ref[...] = dtotal + lax.dot_general(
        later,
        drun,
        (((0,), (0,)), ((), ())),
        precision=exact_mode,
        preferred_element_type=jnp.float32,
    )


def scan_backward(x, dy, bc, run, run_row, dt, dt_row, end, kept, skip, heads):
    length, inner = x.shape
    nstate = bc.shape[1] // 2
    size = STRETCH
    count = length // size
    last = count - 1
    wide = pl.BlockSpec((size, inner), lambda i: (last - i, 0))
    thin = pl.BlockSpec((size, heads), lambda i: (last - i, 0))
    flat = pl.BlockSpec((heads, size), lambda i: (0, last - i))
    both = pl.BlockSpec((size, 2 * nstate), lambda i: (last - i, 0))
    return pl.pallas_call(
        functools.partial(back_kernel, heads),
        grid=(count,),
        out_shape=(
            jax.ShapeDtypeStruct((length, inner), jnp.float32),
            jax.ShapeDtypeStruct((length, 2 * nstate), jnp.float32),
            jax.ShapeDtypeStruct((length, heads), jnp.float32),
            jax.ShapeDtypeStruct((length, heads), jnp.float32),
        ),
        in_specs=[
            wide,
            wide,
            both,
            thin,
            flat,
            thin,
            flat,
            pl.BlockSpec((inner, nstate), lambda i: (0, 0)),
            pl.BlockSpec((1, inner, nstate), lambda i: (last - i, 0, 0)),
            pl.BlockSpec((1, inner), lambda i: (0, 0)),
        ],
        out_specs=(wide, both, thin, thin),
        scratch_shapes=[pltpu.VMEM((inner, nstate), jnp.float32)],
        compiler_params=pltpu.CompilerParams(
            dimension_semantics=("arbitrary",), vmem_limit_bytes=28 * 2**20
        ),
        cost_estimate=pl.CostEstimate(
            flops=40 * 10**9, bytes_accessed=8 * 2**20, transcendentals=2**20
        ),
    )(x, dy, bc, run, run_row, dt, dt_row, end, kept, skip)


def per_device(
    tokens,
    norm_gain,
    gate_weight,
    input_weight,
    state_weight,
    step_weight,
    input_kernel,
    input_offset,
    state_kernel,
    state_offset,
    step_bias,
    decay_log,
    skip_gain,
    gated_gain,
    out_weight,
    cotangent,
):
    ctxn = lax.axis_size("ctx")
    n, tpn = lax.axis_size("dp") * ctxn, lax.axis_size("tp")
    inner, state_width, heads = input_weight.shape[1], state_weight.shape[1], step_weight.shape[1]
    misc_width = -(-(state_width + heads) // LANES) * LANES
    spare = misc_width - state_width - heads
    shard = jnp.concatenate(
        [
            gate_weight,
            input_weight,
            state_weight,
            step_weight,
            jnp.zeros((gate_weight.shape[0], spare), jnp.bfloat16),
            out_weight.T,
        ],
        axis=1,
    )
    full = gather_rows(shard, n, ctxn, 0)
    edges = (0, inner, 2 * inner, 2 * inner + misc_width, 3 * inner + misc_width)
    full_gate, full_input, full_misc, full_out = (
        full[:, low:high] for low, high in zip(edges[:-1], edges[1:])
    )
    residual_in = tokens.astype(jnp.float32)
    normed_low = rms_norm(residual_in, norm_gain).astype(jnp.bfloat16)
    gate_val = jnp.dot(normed_low, full_gate, preferred_element_type=jnp.float32)
    input_pre = jnp.dot(normed_low, full_input, preferred_element_type=jnp.float32)
    misc_pre = jnp.dot(normed_low, full_misc, preferred_element_type=jnp.float32)
    state_pre = misc_pre[:, :state_width]
    step_pre = misc_pre[:, state_width : state_width + heads]
    length = residual_in.shape[0]
    rim_rows = input_kernel.shape[0] - 1
    rim_input, rim_state = shifted(
        (input_pre[length - rim_rows :], state_pre[length - rim_rows :]), "ctx", 1
    )
    values, input_pull = jax.vjp(
        causal_conv, jnp.concatenate([rim_input, input_pre], axis=0), input_kernel, input_offset
    )
    state_act, state_pull = jax.vjp(
        causal_conv, jnp.concatenate([rim_state, state_pre], axis=0), state_kernel, state_offset
    )
    states_all = spread(state_act.astype(jnp.bfloat16), "tp", tpn, 3)
    states_full = jnp.concatenate([states_all[k] for k in range(tpn)], axis=1)
    nstate = states_full.shape[1] // 2
    headdim = inner // heads
    step_sizes = jax.nn.softplus(step_pre + step_bias)
    decays = -step_sizes * jnp.exp(decay_log)
    running = jnp.dot(jnp.tril(jnp.ones((length, length), jnp.float32)), decays, precision=exact_mode)
    starts = jnp.concatenate(
        [jnp.zeros((1, heads), jnp.float32), running[STRETCH - 1 : length - 1 : STRETCH]]
    )
    run = running - jnp.repeat(starts, STRETCH, axis=0)
    run_row, dt_row = run.T, step_sizes.T
    log_decay = running[-1]
    tail = jnp.repeat(jnp.exp(log_decay - running) * step_sizes, headdim, axis=1)
    local_end = over_rows((values * tail).astype(jnp.bfloat16), states_full[:, :nstate])
    incoming = chained(log_decay, local_end, "ctx", forward_chain, False, 4)
    skip_row = jnp.repeat(skip_gain, headdim)[None, :]
    scanned, scaled_low, squares, kept = scan_forward(
        values,
        gate_val,
        states_full,
        run,
        run_row,
        step_sizes,
        dt_row,
        incoming,
        skip_row,
        gated_gain[None, :],
        heads,
    )
    gate_sig = jax.nn.sigmoid(gate_val)
    gate_silu = gate_val * gate_sig
    gated_out = scanned * gate_silu
    partial_out = times_transposed(scaled_low, full_out)
    upstream = cotangent.astype(jnp.float32)
    stats = jnp.stack(
        [squares[:, 0], jnp.sum(upstream * partial_out, axis=1)]
    )
    stats = jnp.sum(spread(stats, "tp", tpn, 1), axis=0)
    projected = lax.psum(partial_out.astype(jnp.bfloat16), "tp").astype(jnp.float32)
    inv_rms = lax.rsqrt(stats[0] / DI + epsilon)
    block_out = (residual_in + inv_rms[:, None] * projected).astype(jnp.bfloat16)
    proj_grad = (inv_rms[:, None] * upstream).astype(jnp.bfloat16)
    rms_grad = -0.5 * inv_rms * inv_rms * inv_rms * stats[1] / DI
    scaled_grad = jnp.dot(proj_grad, full_out, preferred_element_type=jnp.float32)
    grad_gated_gain = jnp.sum(scaled_grad * gated_out, axis=0)
    gated_grad = scaled_grad * gated_gain + 2.0 * rms_grad[:, None] * gated_out
    heads_grad = gated_grad * gate_silu
    gate_grad = gated_grad * scanned * (gate_sig + gate_silu * (1.0 - gate_sig))
    grown = jnp.repeat(jnp.exp(running), headdim, axis=1)
    direct = over_rows((heads_grad * grown).astype(jnp.bfloat16), states_full[:, nstate:])
    chain_grad = chained(log_decay, direct, "ctx", backward_chain, True, 5)
    values_grad, states_grad, step_direct, decays_grad = scan_backward(
        values,
        heads_grad,
        states_full,
        run,
        run_row,
        step_sizes,
        dt_row,
        chain_grad,
        kept,
        skip_row,
        heads,
    )
    skip_grad = jnp.sum(
        jnp.sum(heads_grad * values, axis=0).reshape(heads, headdim), axis=1
    )
    decay_grad = jnp.sum(decays_grad * decays, axis=0)
    step_grad = (step_direct - decays_grad * jnp.exp(decay_log)) * jax.nn.sigmoid(
        step_pre + step_bias
    )
    step_bias_grad = jnp.sum(step_grad, axis=0)
    states_low = states_grad.astype(jnp.bfloat16)
    state_pieces = jnp.stack(
        [states_low[:, k * state_width : (k + 1) * state_width] for k in range(tpn)]
    )
    state_mine = jnp.sum(swap(state_pieces, "tp", tpn, 6).astype(jnp.float32), axis=0)
    input_ext_grad, input_kernel_grad, input_offset_grad = input_pull(values_grad)
    state_ext_grad, state_kernel_grad, state_offset_grad = state_pull(state_mine)
    back_input, back_state = shifted(
        (input_ext_grad[:rim_rows], state_ext_grad[:rim_rows]), "ctx", -1
    )
    input_low = (
        input_ext_grad[rim_rows:] + jnp.pad(back_input, ((length - rim_rows, 0), (0, 0)))
    ).astype(jnp.bfloat16)
    state_low = (
        state_ext_grad[rim_rows:] + jnp.pad(back_state, ((length - rim_rows, 0), (0, 0)))
    ).astype(jnp.bfloat16)
    gate_low = gate_grad.astype(jnp.bfloat16)
    step_low = step_grad.astype(jnp.bfloat16)
    misc_low = jnp.concatenate(
        [state_low, step_low, jnp.zeros((length, spare), jnp.bfloat16)], axis=1
    )
    normed_part = (
        times_transposed(gate_low, full_gate)
        + times_transposed(input_low, full_input)
        + times_transposed(misc_low, full_misc)
    )
    grads = jnp.concatenate(
        [
            over_rows(normed_low, gate_low).astype(jnp.bfloat16),
            over_rows(normed_low, input_low).astype(jnp.bfloat16),
            over_rows(normed_low, misc_low).astype(jnp.bfloat16),
            over_rows(proj_grad, scaled_low).astype(jnp.bfloat16),
        ],
        axis=1,
    )
    inv_in = lax.rsqrt(jnp.mean(residual_in * residual_in, axis=-1, keepdims=True) + epsilon)
    gain_part = jnp.sum(normed_part * (residual_in * inv_in), axis=0)
    pieces = (
        gain_part,
        input_kernel_grad,
        input_offset_grad,
        state_kernel_grad,
        state_offset_grad,
        step_bias_grad,
        decay_grad,
        skip_grad,
        grad_gated_gain,
    )
    count = sum(array.size for array in pieces)
    padded = -(-count // (8 * LANES)) * 8 * LANES
    small = jnp.concatenate(
        [array.reshape(-1) for array in pieces] + [jnp.zeros((padded - count,), jnp.float32)]
    ).reshape(padded // LANES, LANES)
    weight_sums, grad_tokens, small_sum, gain_sum = finish(
        grads,
        normed_part.astype(jnp.bfloat16),
        small,
        tokens,
        cotangent,
        norm_gain,
        n,
        ctxn,
        tpn,
        2,
    )
    small_sum = small_sum.reshape(-1)
    sums, start = [], 0
    for array in pieces:
        sums.append(small_sum[start : start + array.size].reshape(array.shape))
        start += array.size
    misc_start = 2 * inner
    return (
        block_out,
        grad_tokens,
        gain_sum.reshape(-1),
        weight_sums[:, :inner],
        weight_sums[:, inner : 2 * inner],
        weight_sums[:, misc_start : misc_start + state_width],
        weight_sums[:, misc_start + state_width : misc_start + state_width + heads],
        *sums[1:],
        weight_sums[:, edges[3] :].T,
    )


def solution(mesh):
    placed = (
        P(("dp", "ctx"), None),
        P(),
        P(("dp", "ctx"), "tp"),
        P(("dp", "ctx"), "tp"),
        P(("dp", "ctx"), "tp"),
        P(("dp", "ctx"), "tp"),
        P(None, "tp"),
        P("tp"),
        P(None, "tp"),
        P("tp"),
        P("tp"),
        P("tp"),
        P("tp"),
        P("tp"),
        P("tp", ("dp", "ctx")),
        P(("dp", "ctx"), None),
    )
    return jax.shard_map(
        per_device,
        mesh=mesh,
        in_specs=placed,
        out_specs=(
            P(("dp", "ctx"), None),
            P(("dp", "ctx"), None),
            P(),
            P(("dp", "ctx"), "tp"),
            P(("dp", "ctx"), "tp"),
            P(("dp", "ctx"), "tp"),
            P(("dp", "ctx"), "tp"),
            P(None, "tp"),
            P("tp"),
            P(None, "tp"),
            P("tp"),
            P("tp"),
            P("tp"),
            P("tp"),
            P("tp"),
            P("tp", ("dp", "ctx")),
        ),
        check_vma=False,
    )
```

```python
import functools

import jax
import jax.numpy as jnp
from jax import lax
from jax.experimental import pallas as pl
from jax.experimental.pallas import tpu as pltpu
from jax.sharding import PartitionSpec as P

DI = 2048
STRETCH = 256


epsilon = 1e-05
exact_mode = lax.Precision.HIGHEST


def shifted(value, axis, steps):
    count = lax.axis_size(axis)
    leading, last = (max(0, -steps), min(count, count - steps))
    return lax.ppermute(value, axis, [(source, source + steps) for source in range(leading, last)])


def chained(log_decay, state, axis, combine, backward, ident):
    size, here = (lax.axis_size(axis), lax.axis_index(axis))
    rows, nstate = state.shape
    heads = log_decay.shape[0]
    packed = jnp.concatenate(
        [state, jnp.broadcast_to(log_decay[:, None], (heads, nstate)).astype(state.dtype)]
    )
    everything = spread(packed, axis, size, ident).astype(jnp.float32)
    logs = everything[:, rows:, 0]
    states = everything[:, :rows].reshape(size, heads, rows // heads, nstate)
    before = (jnp.zeros((heads,), jnp.float32), jnp.zeros(states.shape[1:], jnp.float32))
    for k in range(size):
        at = size - 1 - k if backward else k
        reached = at > here if backward else at < here
        new = combine(before, (logs[at], states[at]))
        before = jax.tree.map(lambda a, b: jnp.where(reached, a, b), new, before)
    return before[1].reshape(rows, nstate)


def rms_norm(values, norm_scale):
    meansq = jnp.mean(values * values, axis=-1, keepdims=True)
    return values * lax.rsqrt(meansq + epsilon) * norm_scale


def causal_conv(padded, kernel, offset):
    tap_count = kernel.shape[0]
    length = padded.shape[0] - tap_count + 1
    summed = offset[None, :] + kernel[0][None, :] * padded[0:length]
    for tap_index in range(1, tap_count):
        summed = summed + kernel[tap_index][None, :] * padded[tap_index : tap_index + length]
    return jax.nn.silu(summed)


def forward_chain(earlier, later):
    return (earlier[0] + later[0], jnp.exp(later[0])[:, None, None] * earlier[1] + later[1])


def backward_chain(earlier, later):
    return (earlier[0] + later[0], later[1] + jnp.exp(later[0])[:, None, None] * earlier[1])


def times_transposed(left_side, right_side):
    return lax.dot_general(
        left_side, right_side, (((1,), (1,)), ((), ())), preferred_element_type=jnp.float32
    )


def over_rows(left_side, right_side):
    return lax.dot_general(
        left_side, right_side, (((0,), (0,)), ((), ())), preferred_element_type=jnp.float32
    )


MESH = pl.DeviceIdType.MESH
LANES = 128


def line_up(peers):
    barrier = pltpu.get_barrier_semaphore()
    for peer in peers:
        pl.semaphore_signal(barrier, inc=1, device_id=peer, device_id_type=MESH)
    pl.semaphore_wait(barrier, len(peers))


def send_to(source, target, sends, recvs, peer):
    return pltpu.make_async_remote_copy(
        src_ref=source,
        dst_ref=target,
        send_sem=sends,
        recv_sem=recvs,
        device_id=peer,
        device_id_type=MESH,
    )


def gather_kernel(n, ctxn, x_ref, full_ref, own_sem, send, recv, fsend, frecv):
    here = lax.axis_index("dp") * ctxn + lax.axis_index("ctx")
    half = n // 2
    chip, core = lax.div(here, 2), lax.rem(here, 2)
    rows = x_ref.shape[0]

    def spot(index):
        return {"dp": lax.div(index, ctxn), "ctx": lax.rem(index, ctxn)}

    def at(index):
        return full_ref.at[pl.ds(pl.multiple_of(index * rows, rows), rows)]

    sibling = spot(2 * chip + 1 - core)
    peers = [spot(2 * lax.rem(chip + step, half) + core) for step in range(1, half)]
    line_up([sibling] + peers)
    copies = []
    for step in range(1, half):
        copy = send_to(x_ref, at(here), send.at[step], recv.at[step], peers[step - 1])
        copy.start()
        copies.append(copy)
    beside = send_to(x_ref, at(here), send.at[0], recv.at[0], sibling)
    beside.start()
    own = pltpu.make_async_copy(x_ref, at(here), own_sem)
    own.start()
    passed = []
    for step in range(1, half):
        origin = 2 * lax.rem(chip + half - step, half) + core
        copies[step - 1].wait_recv()
        copy = send_to(at(origin), at(origin), fsend.at[step], frecv.at[step], sibling)
        copy.start()
        passed.append(copy)
    own.wait()
    beside.wait()
    for copy in copies:
        copy.wait_send()
    for copy in passed:
        copy.wait()


def gather_rows(shard, n, ctxn, ident):
    rows, columns = shard.shape
    half = n // 2
    return pl.pallas_call(
        functools.partial(gather_kernel, n, ctxn),
        out_shape=jax.ShapeDtypeStruct((n * rows, columns), shard.dtype),
        in_specs=[pl.BlockSpec(memory_space=pltpu.VMEM)],
        out_specs=pl.BlockSpec(memory_space=pltpu.VMEM),
        scratch_shapes=[pltpu.SemaphoreType.DMA] + [pltpu.SemaphoreType.DMA((half,))] * 4,
        compiler_params=pltpu.CompilerParams(
            collective_id=ident, has_side_effects=True, vmem_limit_bytes=10 * 2**20
        ),
    )(shard)


def spread_kernel(axis, n, x_ref, all_ref, own_sem, send, recv):
    here = lax.axis_index(axis)
    peers = [{axis: lax.rem(here + step, n)} for step in range(1, n)]
    line_up(peers)
    copies = []
    for step in range(1, n):
        copy = send_to(x_ref, all_ref.at[here], send.at[step], recv.at[step], peers[step - 1])
        copy.start()
        copies.append(copy)
    own = pltpu.make_async_copy(x_ref, all_ref.at[here], own_sem)
    own.start()
    own.wait()
    for copy in copies:
        copy.wait()


def spread(array, axis, n, ident):
    return pl.pallas_call(
        functools.partial(spread_kernel, axis, n),
        out_shape=jax.ShapeDtypeStruct((n,) + array.shape, array.dtype),
        in_specs=[pl.BlockSpec(memory_space=pltpu.VMEM)],
        out_specs=pl.BlockSpec(memory_space=pltpu.VMEM),
        scratch_shapes=[pltpu.SemaphoreType.DMA] + [pltpu.SemaphoreType.DMA((n,))] * 2,
        compiler_params=pltpu.CompilerParams(
            collective_id=ident, has_side_effects=True, vmem_limit_bytes=10 * 2**20
        ),
    )(array)


def finish_kernel(
    n,
    ctxn,
    tpn,
    grads_ref,
    part_ref,
    small_ref,
    tokens_ref,
    cot_ref,
    gain_ref,
    dw_ref,
    gt_ref,
    sum_ref,
    total_ref,
    beside_buf,
    out_buf,
    in_buf,
    small_in,
    gain_out,
    gain_in,
    tp_in,
    tp_out,
    tp_all,
    sems,
    small_sems,
    tp_sems,
):
    here = lax.axis_index("dp") * ctxn + lax.axis_index("ctx")
    mine = lax.axis_index("tp")
    half = n // 2
    chip, core = lax.div(here, 2), lax.rem(here, 2)
    rows = dw_ref.shape[0]
    piece = tp_out.shape[0]

    def spot(index):
        return {"dp": lax.div(index, ctxn), "ctx": lax.rem(index, ctxn)}

    def span(index):
        return pl.ds(pl.multiple_of(index * rows, rows), rows)

    def part(index):
        return pl.ds(pl.multiple_of(index * piece, piece), piece)

    sibling = spot(2 * chip + 1 - core)
    group = [spot(lax.rem(here + step, n)) for step in range(1, n)]
    line = [{"tp": lax.rem(mine + step, tpn)} for step in range(1, tpn)]
    line_up(group + line)

    scatter = []
    for step in range(1, tpn):
        copy = send_to(
            part_ref.at[part(lax.rem(mine + step, tpn))],
            tp_in.at[step],
            tp_sems.at[0, step],
            tp_sems.at[1, step],
            line[step - 1],
        )
        copy.start()
        scatter.append(copy)
    beside = []
    for step in list(range(1, half)) + [0]:
        copy = send_to(
            grads_ref.at[span(2 * lax.rem(chip + step, half) + 1 - core)],
            beside_buf.at[step],
            sems.at[0, step],
            sems.at[1, step],
            sibling,
        )
        copy.start()
        beside.append(copy)
    smalls = []
    for step in range(1, n):
        copy = send_to(
            small_ref, small_in.at[here], small_sems.at[0, step], small_sems.at[1, step], group[step - 1]
        )
        copy.start()
        smalls.append(copy)
    small_in[here] = small_ref[...]

    across = []
    for step in range(1, half):
        target = 2 * lax.rem(chip + step, half) + core
        beside[step - 1].wait_recv()
        out_buf[step] = (
            grads_ref[span(target)].astype(jnp.float32) + beside_buf[step].astype(jnp.float32)
        ).astype(jnp.bfloat16)
        copy = send_to(
            out_buf.at[step], in_buf.at[step], sems.at[2, step], sems.at[3, step], spot(target)
        )
        copy.start()
        across.append(copy)
    beside[half - 1].wait_recv()
    dw_ref[...] = grads_ref[span(here)].astype(jnp.float32) + beside_buf[0].astype(jnp.float32)

    for copy in smalls:
        copy.wait_recv()
    total = small_in[0]
    for index in range(1, n):
        total = total + small_in[index]
    sum_ref[...] = total
    gain_out[...] = total[:8]
    gain_in[mine] = total[:8]
    gains = []
    for step in range(1, tpn):
        copy = send_to(
            gain_out, gain_in.at[mine], tp_sems.at[4, step], tp_sems.at[5, step], line[step - 1]
        )
        copy.start()
        gains.append(copy)

    normed_grad = part_ref[part(mine)].astype(jnp.float32)
    for step in range(1, tpn):
        scatter[step - 1].wait_recv()
        normed_grad = normed_grad + tp_in[step].astype(jnp.float32)
    tokens = tokens_ref[part(mine)].astype(jnp.float32)
    inv = lax.rsqrt(jnp.mean(tokens * tokens, axis=-1, keepdims=True) + epsilon)
    scaled = normed_grad * gain_ref[...]
    along = jnp.mean(scaled * tokens, axis=-1, keepdims=True)
    change = (inv * scaled - tokens * (inv * inv * inv * along)).astype(jnp.bfloat16)
    tp_out[...] = change
    collect = []
    for step in range(1, tpn):
        copy = send_to(
            tp_out, tp_all.at[part(mine)], tp_sems.at[2, step], tp_sems.at[3, step], line[step - 1]
        )
        copy.start()
        collect.append(copy)
    gt_ref[part(mine)] = cot_ref[part(mine)].astype(jnp.float32) + change.astype(jnp.float32)

    for step in range(1, half):
        across[step - 1].wait_recv()
        dw_ref[...] += in_buf[step].astype(jnp.float32)
    for copy in gains:
        copy.wait_recv()
    whole = gain_in[0]
    for index in range(1, tpn):
        whole = whole + gain_in[index]
    total_ref[...] = whole
    for step in range(1, tpn):
        collect[step - 1].wait_recv()
        where = part(lax.rem(mine + tpn - step, tpn))
        gt_ref[where] = cot_ref[where].astype(jnp.float32) + tp_all[where].astype(jnp.float32)
    for copy in scatter + beside + smalls + across + gains + collect:
        copy.wait_send()


def finish(grads, part, small, tokens, cotangent, norm_gain, n, ctxn, tpn, ident):
    rows, columns = grads.shape[0] // n, grads.shape[1]
    length, width = tokens.shape
    half = n // 2
    piece = length // tpn
    return pl.pallas_call(
        functools.partial(finish_kernel, n, ctxn, tpn),
        out_shape=(
            jax.ShapeDtypeStruct((rows, columns), jnp.float32),
            jax.ShapeDtypeStruct((length, width), jnp.float32),
            jax.ShapeDtypeStruct(small.shape, jnp.float32),
            jax.ShapeDtypeStruct((8, LANES), jnp.float32),
        ),
        in_specs=[pl.BlockSpec(memory_space=pltpu.VMEM)] * 6,
        out_specs=(pl.BlockSpec(memory_space=pltpu.VMEM),) * 4,
        scratch_shapes=[
            pltpu.VMEM((half, rows, columns), jnp.bfloat16),
            pltpu.VMEM((half, rows, columns), jnp.bfloat16),
            pltpu.VMEM((half, rows, columns), jnp.bfloat16),
            pltpu.VMEM((n,) + small.shape, jnp.float32),
            pltpu.VMEM((8, LANES), jnp.float32),
            pltpu.VMEM((tpn, 8, LANES), jnp.float32),
            pltpu.VMEM((tpn, piece, width), jnp.bfloat16),
            pltpu.VMEM((piece, width), jnp.bfloat16),
            pltpu.VMEM((length, width), jnp.bfloat16),
            pltpu.SemaphoreType.DMA((4, half)),
            pltpu.SemaphoreType.DMA((2, n)),
            pltpu.SemaphoreType.DMA((6, tpn)),
        ],
        compiler_params=pltpu.CompilerParams(
            collective_id=ident, has_side_effects=True, vmem_limit_bytes=28 * 2**20
        ),
    )(grads, part, small, tokens, cotangent, norm_gain.reshape(1, width))


def swap_kernel(axis, n, x_ref, all_ref, own_sem, send, recv):
    here = lax.axis_index(axis)
    peers = [{axis: lax.rem(here + step, n)} for step in range(1, n)]
    line_up(peers)
    copies = []
    for step in range(1, n):
        copy = send_to(
            x_ref.at[lax.rem(here + step, n)],
            all_ref.at[here],
            send.at[step],
            recv.at[step],
            peers[step - 1],
        )
        copy.start()
        copies.append(copy)
    own = pltpu.make_async_copy(x_ref.at[here], all_ref.at[here], own_sem)
    own.start()
    own.wait()
    for copy in copies:
        copy.wait()


def swap(array, axis, n, ident):
    return pl.pallas_call(
        functools.partial(swap_kernel, axis, n),
        out_shape=jax.ShapeDtypeStruct(array.shape, array.dtype),
        in_specs=[pl.BlockSpec(memory_space=pltpu.VMEM)],
        out_specs=pl.BlockSpec(memory_space=pltpu.VMEM),
        scratch_shapes=[pltpu.SemaphoreType.DMA] + [pltpu.SemaphoreType.DMA((n,))] * 2,
        compiler_params=pltpu.CompilerParams(
            collective_id=ident, has_side_effects=True, vmem_limit_bytes=10 * 2**20
        ),
    )(array)


def mm(left, right, dims):
    return lax.dot_general(left, right, (dims, ((), ())), preferred_element_type=jnp.float32)


def widen(columns, width):
    rows, heads = columns.shape
    return jnp.concatenate(
        [jnp.broadcast_to(columns[:, h : h + 1], (rows, width)) for h in range(heads)], axis=1
    )


def tallen(row, width, lanes):
    return jnp.concatenate(
        [jnp.broadcast_to(row[:, h : h + 1], (width, lanes)) for h in range(row.shape[1])], axis=0
    )


def per_head(wide, heads):
    width = wide.shape[1] // heads
    return jnp.concatenate(
        [
            jnp.sum(wide[:, h * width : (h + 1) * width], axis=1, keepdims=True)
            for h in range(heads)
        ],
        axis=1,
    )


def decay_matrix(run, run_row, h, causal):
    return jnp.exp(jnp.where(causal, run[:, h : h + 1] - run_row[h : h + 1, :], -1e30))


def causal_mask(size):
    down = lax.broadcasted_iota(jnp.int32, (size, size), 0)
    right = lax.broadcasted_iota(jnp.int32, (size, size), 1)
    return down >= right


def scan_kernel(
    heads,
    x_ref,
    gate_ref,
    bc_ref,
    run_ref,
    run_row_ref,
    dt_ref,
    dt_row_ref,
    start_ref,
    skip_ref,
    gain_ref,
    scanned_ref,
    scaled_ref,
    square_ref,
    kept_ref,
    state,
):
    low = jnp.bfloat16

    @pl.when(pl.program_id(0) == 0)
    def _():
        state[...] = start_ref[...]

    size, inner = x_ref.shape
    width = inner // heads
    nstate = bc_ref.shape[1] // 2
    b, c = bc_ref[:, :nstate], bc_ref[:, nstate:]
    run, run_row = run_ref[...], run_row_ref[...]
    x = x_ref[...]
    x_low = x.astype(low)
    causal = causal_mask(size)
    scores = mm(c, b, ((1,), (1,)))
    held = state[...].astype(low)
    kept_ref[0] = held
    carried = mm(c, held, ((1,), (1,))) * widen(jnp.exp(run), width)
    within = []
    for h in range(heads):
        mixing = decay_matrix(run, run_row, h, causal) * scores * dt_row_ref[h : h + 1, :]
        within.append(mm(mixing.astype(low), x_low[:, h * width : (h + 1) * width], ((1,), (0,))))
    scanned = carried + jnp.concatenate(within, axis=1) + skip_ref[...] * x
    scanned_ref[...] = scanned
    total = run[size - 1 :, :]
    tail = jnp.exp(total - run) * dt_ref[...]
    fresh = mm((x * widen(tail, width)).astype(low), b, ((0,), (0,)))
    state[...] = tallen(jnp.exp(total), width, nstate) * state[...] + fresh
    gate = gate_ref[...]
    gated = scanned * (gate * jax.nn.sigmoid(gate))
    scaled_ref[...] = (gated * gain_ref[...]).astype(low)
    square_ref[...] = jnp.sum(gated * gated, axis=1, keepdims=True)


def scan_forward(x, gate, bc, run, run_row, dt, dt_row, start, skip, gain, heads):
    length, inner = x.shape
    nstate = bc.shape[1] // 2
    size = STRETCH
    wide = pl.BlockSpec((size, inner), lambda i: (i, 0))
    thin = pl.BlockSpec((size, heads), lambda i: (i, 0))
    flat = pl.BlockSpec((heads, size), lambda i: (0, i))
    row = pl.BlockSpec((1, inner), lambda i: (0, 0))
    return pl.pallas_call(
        functools.partial(scan_kernel, heads),
        grid=(length // size,),
        out_shape=(
            jax.ShapeDtypeStruct((length, inner), jnp.float32),
            jax.ShapeDtypeStruct((length, inner), jnp.bfloat16),
            jax.ShapeDtypeStruct((length, 1), jnp.float32),
            jax.ShapeDtypeStruct((length // size, inner, nstate), jnp.bfloat16),
        ),
        in_specs=[
            wide,
            wide,
            pl.BlockSpec((size, 2 * nstate), lambda i: (i, 0)),
            thin,
            flat,
            thin,
            flat,
            pl.BlockSpec((inner, nstate), lambda i: (0, 0)),
            row,
            row,
        ],
        out_specs=(
            wide,
            wide,
            pl.BlockSpec((size, 1), lambda i: (i, 0)),
            pl.BlockSpec((1, inner, nstate), lambda i: (i, 0, 0)),
        ),
        scratch_shapes=[pltpu.VMEM((inner, nstate), jnp.float32)],
        compiler_params=pltpu.CompilerParams(
            dimension_semantics=("arbitrary",), vmem_limit_bytes=28 * 2**20
        ),
    )(x, gate, bc, run, run_row, dt, dt_row, start, skip, gain)


def back_kernel(
    heads,
    x_ref,
    dy_ref,
    bc_ref,
    run_ref,
    run_row_ref,
    dt_ref,
    dt_row_ref,
    end_ref,
    kept_ref,
    skip_ref,
    dx_ref,
    dbc_ref,
    ddt_ref,
    ddecay_ref,
    state,
):
    low = jnp.bfloat16

    @pl.when(pl.program_id(0) == 0)
    def _():
        state[...] = end_ref[...]

    size, inner = x_ref.shape
    width = inner // heads
    nstate = bc_ref.shape[1] // 2
    b, c = bc_ref[:, :nstate], bc_ref[:, nstate:]
    run, run_row, dt = run_ref[...], run_row_ref[...], dt_ref[...]
    x, dy = x_ref[...], dy_ref[...]
    x_low, dy_low = x.astype(low), dy.astype(low)
    causal = causal_mask(size)
    scores = mm(c, b, ((1,), (1,)))
    held = kept_ref[0]
    ds = state[...]
    ds_low = ds.astype(low)

    grown = widen(jnp.exp(run), width)
    dy_grown = dy * grown
    dy_grown_low = dy_grown.astype(low)
    drun = per_head(dy_grown * mm(c, held, ((1,), (1,))), heads)
    dc = mm(dy_grown_low, held, ((1,), (0,)))
    total = run[size - 1 :, :]
    left = jnp.exp(total - run)
    fade = widen(left, width)
    spare = widen(left * dt, width)
    pulled = mm(b, ds_low, ((1,), (1,)))
    db = mm((x * spare).astype(low), ds_low, ((1,), (0,)))
    tail_grad = per_head(x * fade * pulled, heads)
    out_tail = tail_grad * dt
    drun = drun - out_tail
    shrink = tallen(jnp.exp(total), width, nstate)
    lost = jnp.sum(shrink * ds * held.astype(jnp.float32), axis=1, keepdims=True)
    dtotal = jnp.concatenate(
        [
            jnp.sum(lost[h * width : (h + 1) * width], axis=0, keepdims=True)
            for h in range(heads)
        ],
        axis=1,
    ) + jnp.sum(out_tail, axis=0, keepdims=True)
    state[...] = shrink * ds + mm(dy_grown_low, c, ((0,), (0,)))

    dscores = jnp.zeros((size, size), jnp.float32)
    rows, columns, dx = [], [], []
    for h in range(heads):
        lanes = slice(h * width, (h + 1) * width)
        fall = decay_matrix(run, run_row, h, causal)
        dt_row = dt_row_ref[h : h + 1, :]
        products = mm(dy_low[:, lanes], x_low[:, lanes], ((1,), (1,))) * fall
        dscores = dscores + products * dt_row
        terms = products * scores
        columns.append(jnp.sum(terms, axis=0, keepdims=True))
        rows.append(jnp.sum(terms * dt_row, axis=1, keepdims=True))
        mixing = (fall * scores * dt_row).astype(low)
        dx.append(mm(mixing, dy_low[:, lanes], ((0,), (0,))))
    dx_ref[...] = jnp.concatenate(dx, axis=1) + spare * pulled + skip_ref[...] * dy
    dscores = dscores.astype(low)
    dbc_ref[:, :nstate] = db + mm(dscores, c, ((0,), (0,)))
    dbc_ref[:, nstate:] = dc + mm(dscores, b, ((1,), (0,)))
    column = jnp.concatenate(columns, axis=0).T
    ddt_ref[...] = column + tail_grad
    drun = drun + jnp.concatenate(rows, axis=1) - column * dt
    later = jnp.where(causal, 1.0, 0.0)
    ddecay_ref[...] = dtotal + lax.dot_general(
        later,
        drun,
        (((0,), (0,)), ((), ())),
        precision=exact_mode,
        preferred_element_type=jnp.float32,
    )


def scan_backward(x, dy, bc, run, run_row, dt, dt_row, end, kept, skip, heads):
    length, inner = x.shape
    nstate = bc.shape[1] // 2
    size = STRETCH
    count = length // size
    last = count - 1
    wide = pl.BlockSpec((size, inner), lambda i: (last - i, 0))
    thin = pl.BlockSpec((size, heads), lambda i: (last - i, 0))
    flat = pl.BlockSpec((heads, size), lambda i: (0, last - i))
    both = pl.BlockSpec((size, 2 * nstate), lambda i: (last - i, 0))
    return pl.pallas_call(
        functools.partial(back_kernel, heads),
        grid=(count,),
        out_shape=(
            jax.ShapeDtypeStruct((length, inner), jnp.float32),
            jax.ShapeDtypeStruct((length, 2 * nstate), jnp.float32),
            jax.ShapeDtypeStruct((length, heads), jnp.float32),
            jax.ShapeDtypeStruct((length, heads), jnp.float32),
        ),
        in_specs=[
            wide,
            wide,
            both,
            thin,
            flat,
            thin,
            flat,
            pl.BlockSpec((inner, nstate), lambda i: (0, 0)),
            pl.BlockSpec((1, inner, nstate), lambda i: (last - i, 0, 0)),
            pl.BlockSpec((1, inner), lambda i: (0, 0)),
        ],
        out_specs=(wide, both, thin, thin),
        scratch_shapes=[pltpu.VMEM((inner, nstate), jnp.float32)],
        compiler_params=pltpu.CompilerParams(
            dimension_semantics=("arbitrary",), vmem_limit_bytes=28 * 2**20
        ),
        cost_estimate=pl.CostEstimate(
            flops=40 * 10**9, bytes_accessed=8 * 2**20, transcendentals=2**20
        ),
    )(x, dy, bc, run, run_row, dt, dt_row, end, kept, skip)


def per_device(
    tokens,
    norm_gain,
    gate_weight,
    input_weight,
    state_weight,
    step_weight,
    input_kernel,
    input_offset,
    state_kernel,
    state_offset,
    step_bias,
    decay_log,
    skip_gain,
    gated_gain,
    out_weight,
    cotangent,
):
    ctxn = lax.axis_size("ctx")
    n, tpn = lax.axis_size("dp") * ctxn, lax.axis_size("tp")
    inner, state_width, heads = input_weight.shape[1], state_weight.shape[1], step_weight.shape[1]
    misc_width = -(-(state_width + heads) // LANES) * LANES
    spare = misc_width - state_width - heads
    shard = jnp.concatenate(
        [
            gate_weight,
            input_weight,
            state_weight,
            step_weight,
            jnp.zeros((gate_weight.shape[0], spare), jnp.bfloat16),
            out_weight.T,
        ],
        axis=1,
    )
    full = gather_rows(shard, n, ctxn, 0)
    edges = (0, inner, 2 * inner, 2 * inner + misc_width, 3 * inner + misc_width)
    full_gate, full_input, full_misc, full_out = (
        full[:, low:high] for low, high in zip(edges[:-1], edges[1:])
    )
    residual_in = tokens.astype(jnp.float32)
    normed_low = rms_norm(residual_in, norm_gain).astype(jnp.bfloat16)
    gate_val = jnp.dot(normed_low, full_gate, preferred_element_type=jnp.float32)
    input_pre = jnp.dot(normed_low, full_input, preferred_element_type=jnp.float32)
    misc_pre = jnp.dot(normed_low, full_misc, preferred_element_type=jnp.float32)
    state_pre = misc_pre[:, :state_width]
    step_pre = misc_pre[:, state_width : state_width + heads]
    length = residual_in.shape[0]
    rim_rows = input_kernel.shape[0] - 1
    rim_input, rim_state = shifted(
        (input_pre[length - rim_rows :], state_pre[length - rim_rows :]), "ctx", 1
    )
    values, input_pull = jax.vjp(
        causal_conv, jnp.concatenate([rim_input, input_pre], axis=0), input_kernel, input_offset
    )
    state_act, state_pull = jax.vjp(
        causal_conv, jnp.concatenate([rim_state, state_pre], axis=0), state_kernel, state_offset
    )
    half_length = length // 2
    state_low_act = state_act.astype(jnp.bfloat16)
    states_all = spread(
        jnp.concatenate([state_low_act[:half_length], state_low_act[half_length:]], axis=1),
        "tp",
        tpn,
        3,
    )
    states_full = jnp.concatenate(
        [
            jnp.concatenate([states_all[k, :, low:high] for k in range(tpn)], axis=1)
            for low, high in ((0, state_width), (state_width, 2 * state_width))
        ],
        axis=0,
    )
    nstate = states_full.shape[1] // 2
    headdim = inner // heads
    step_sizes = jax.nn.softplus(step_pre + step_bias)
    decays = -step_sizes * jnp.exp(decay_log)
    running = jnp.dot(jnp.tril(jnp.ones((length, length), jnp.float32)), decays, precision=exact_mode)
    starts = jnp.concatenate(
        [jnp.zeros((1, heads), jnp.float32), running[STRETCH - 1 : length - 1 : STRETCH]]
    )
    run = running - jnp.repeat(starts, STRETCH, axis=0)
    run_row, dt_row = run.T, step_sizes.T
    log_decay = running[-1]
    members = jnp.where(
        lax.broadcasted_iota(jnp.int32, (heads, inner), 1) // headdim
        == lax.broadcasted_iota(jnp.int32, (heads, inner), 0),
        1.0,
        0.0,
    )
    tail = jnp.dot(jnp.exp(log_decay - running) * step_sizes, members, precision=exact_mode)
    local_end = over_rows((values * tail).astype(jnp.bfloat16), states_full[:, :nstate])
    incoming = chained(log_decay, local_end, "ctx", forward_chain, False, 4)
    skip_row = jnp.repeat(skip_gain, headdim)[None, :]
    scanned, scaled_low, squares, kept = scan_forward(
        values,
        gate_val,
        states_full,
        run,
        run_row,
        step_sizes,
        dt_row,
        incoming,
        skip_row,
        gated_gain[None, :],
        heads,
    )
    gate_sig = jax.nn.sigmoid(gate_val)
    gate_silu = gate_val * gate_sig
    gated_out = scanned * gate_silu
    partial_out = times_transposed(scaled_low, full_out)
    upstream = cotangent.astype(jnp.float32)
    stats = jnp.stack(
        [squares[:, 0], jnp.sum(upstream * partial_out, axis=1)]
    )
    stats = jnp.sum(spread(stats, "tp", tpn, 1), axis=0)
    projected = lax.psum_scatter(
        partial_out.astype(jnp.bfloat16), "tp", scatter_dimension=0, tiled=True
    ).astype(jnp.float32)
    inv_rms = lax.rsqrt(stats[0] / DI + epsilon)
    piece = length // tpn
    first = lax.axis_index("tp") * piece
    block_piece = (
        lax.dynamic_slice_in_dim(tokens, first, piece).astype(jnp.float32)
        + lax.dynamic_slice_in_dim(inv_rms, first, piece)[:, None] * projected
    ).astype(jnp.bfloat16)
    proj_grad = (inv_rms[:, None] * upstream).astype(jnp.bfloat16)
    rms_grad = -0.5 * inv_rms * inv_rms * inv_rms * stats[1] / DI
    scaled_grad = jnp.dot(proj_grad, full_out, preferred_element_type=jnp.float32)
    grad_gated_gain = jnp.sum(scaled_grad * gated_out, axis=0)
    gated_grad = scaled_grad * gated_gain + 2.0 * rms_grad[:, None] * gated_out
    heads_grad = gated_grad * gate_silu
    gate_grad = gated_grad * scanned * (gate_sig + gate_silu * (1.0 - gate_sig))
    grown = jnp.dot(jnp.exp(running), members, precision=exact_mode)
    direct = over_rows((heads_grad * grown).astype(jnp.bfloat16), states_full[:, nstate:])
    chain_grad = chained(log_decay, direct, "ctx", backward_chain, True, 5)
    values_grad, states_grad, step_direct, decays_grad = scan_backward(
        values,
        heads_grad,
        states_full,
        run,
        run_row,
        step_sizes,
        dt_row,
        chain_grad,
        kept,
        skip_row,
        heads,
    )
    skip_grad = jnp.sum(
        jnp.sum(heads_grad * values, axis=0).reshape(heads, headdim), axis=1
    )
    decay_grad = jnp.sum(decays_grad * decays, axis=0)
    step_grad = (step_direct - decays_grad * jnp.exp(decay_log)) * jax.nn.sigmoid(
        step_pre + step_bias
    )
    step_bias_grad = jnp.sum(step_grad, axis=0)
    states_grad, block_piece = lax.optimization_barrier((states_grad, block_piece))
    block_out = lax.all_gather(block_piece, "tp", axis=0, tiled=True)
    states_low = states_grad.astype(jnp.bfloat16)
    state_pieces = jnp.stack(
        [
            jnp.concatenate([owned[:half_length], owned[half_length:]], axis=1)
            for owned in (
                states_low[:, k * state_width : (k + 1) * state_width] for k in range(tpn)
            )
        ]
    )
    state_sum = jnp.sum(swap(state_pieces, "tp", tpn, 6).astype(jnp.float32), axis=0)
    state_mine = jnp.concatenate([state_sum[:, :state_width], state_sum[:, state_width:]], axis=0)
    input_ext_grad, input_kernel_grad, input_offset_grad = input_pull(values_grad)
    state_ext_grad, state_kernel_grad, state_offset_grad = state_pull(state_mine)
    back_input, back_state = shifted(
        (input_ext_grad[:rim_rows], state_ext_grad[:rim_rows]), "ctx", -1
    )
    input_low = (
        input_ext_grad[rim_rows:] + jnp.pad(back_input, ((length - rim_rows, 0), (0, 0)))
    ).astype(jnp.bfloat16)
    state_low = (
        state_ext_grad[rim_rows:] + jnp.pad(back_state, ((length - rim_rows, 0), (0, 0)))
    ).astype(jnp.bfloat16)
    gate_low = gate_grad.astype(jnp.bfloat16)
    step_low = step_grad.astype(jnp.bfloat16)
    misc_low = jnp.concatenate(
        [state_low, step_low, jnp.zeros((length, spare), jnp.bfloat16)], axis=1
    )
    normed_part = (
        times_transposed(gate_low, full_gate)
        + times_transposed(input_low, full_input)
        + times_transposed(misc_low, full_misc)
    )
    grads = jnp.concatenate(
        [
            over_rows(normed_low, gate_low).astype(jnp.bfloat16),
            over_rows(normed_low, input_low).astype(jnp.bfloat16),
            over_rows(normed_low, misc_low).astype(jnp.bfloat16),
            over_rows(proj_grad, scaled_low).astype(jnp.bfloat16),
        ],
        axis=1,
    )
    inv_in = lax.rsqrt(jnp.mean(residual_in * residual_in, axis=-1, keepdims=True) + epsilon)
    gain_part = jnp.sum(normed_part * (residual_in * inv_in), axis=0)
    pieces = (
        gain_part,
        input_kernel_grad,
        input_offset_grad,
        state_kernel_grad,
        state_offset_grad,
        step_bias_grad,
        decay_grad,
        skip_grad,
        grad_gated_gain,
    )
    count = sum(array.size for array in pieces)
    padded = -(-count // (8 * LANES)) * 8 * LANES
    small = jnp.concatenate(
        [array.reshape(-1) for array in pieces] + [jnp.zeros((padded - count,), jnp.float32)]
    ).reshape(padded // LANES, LANES)
    weight_sums, grad_tokens, small_sum, gain_sum = finish(
        grads,
        normed_part.astype(jnp.bfloat16),
        small,
        tokens,
        cotangent,
        norm_gain,
        n,
        ctxn,
        tpn,
        2,
    )
    small_sum = small_sum.reshape(-1)
    sums, start = [], 0
    for array in pieces:
        sums.append(small_sum[start : start + array.size].reshape(array.shape))
        start += array.size
    misc_start = 2 * inner
    return (
        block_out,
        grad_tokens,
        gain_sum.reshape(-1),
        weight_sums[:, :inner],
        weight_sums[:, inner : 2 * inner],
        weight_sums[:, misc_start : misc_start + state_width],
        weight_sums[:, misc_start + state_width : misc_start + state_width + heads],
        *sums[1:],
        weight_sums[:, edges[3] :].T,
    )


def solution(mesh):
    placed = (
        P(("dp", "ctx"), None),
        P(),
        P(("dp", "ctx"), "tp"),
        P(("dp", "ctx"), "tp"),
        P(("dp", "ctx"), "tp"),
        P(("dp", "ctx"), "tp"),
        P(None, "tp"),
        P("tp"),
        P(None, "tp"),
        P("tp"),
        P("tp"),
        P("tp"),
        P("tp"),
        P("tp"),
        P("tp", ("dp", "ctx")),
        P(("dp", "ctx"), None),
    )
    return jax.shard_map(
        per_device,
        mesh=mesh,
        in_specs=placed,
        out_specs=(
            P(("dp", "ctx"), None),
            P(("dp", "ctx"), None),
            P(),
            P(("dp", "ctx"), "tp"),
            P(("dp", "ctx"), "tp"),
            P(("dp", "ctx"), "tp"),
            P(("dp", "ctx"), "tp"),
            P(None, "tp"),
            P("tp"),
            P(None, "tp"),
            P("tp"),
            P("tp"),
            P("tp"),
            P("tp"),
            P("tp"),
            P("tp", ("dp", "ctx")),
        ),
        check_vma=False,
    )
```
